128 devices in a mesh: grp: 4 (over z), sfc: 32 (over y, x, core).
Axes of the slice: x: 4, y: 4, z: 4, core: 2. Of those that a mesh axis runs over, the one named last changes fastest.
Arguments:
- coarse_state: float32 [384, 5, 32, 1024], P(('grp', 'sfc')), may hold values from -6 to 6
- fine_old: float32 [1280, 5, 32, 1024], P(('grp', 'sfc')), may hold values from -6 to 6
- coarse_owner: int32 [256], replicated, may hold values from 0 to 127, as said below
- fine_owner_old: int32 [1024], replicated, may hold values from 0 to 127, as said below
- fine_owner_new: int32 [1024], replicated, may hold values from 0 to 127, as said below
- fine_nbr: int32 [1024, 6], replicated, may hold values from -1 to 1023, as said below
- reflux_map: int32 [1024, 3], replicated, may hold values from -1 to 254, as said below
Outputs:
- coarse_out: float32 [384, 5, 32, 1024], P(('grp', 'sfc'))
- fine_new: float32 [1792, 5, 32, 1024], P(('grp', 'sfc'))
The draws below stay inside these ranges and needn't reach their ends.
Inputs may be any that keep to these rules, and one draw needn't show every extreme that they name: `coarse_owner`: Non-decreasing; each device holds 1 to 3 coarse patches, and some device holds 3. `fine_owner_old`: Non-decreasing; each device holds 6 to 10 fine patches. `fine_owner_new`: Non-decreasing; each device holds 3 to 14 fine patches. Along the index over grp and sfc together, each patch's new owner is its old owner or the device next to it, and at most 2 patches go from one device to each side. The owners of a fine patch, of its neighbours and of its reflux target's coarse patch are at most two devices apart. `fine_nbr`: patches 8k to 8k + 7 refine coarse patch 2k + 1 as a 2 x 2 x 2 block in an order drawn per block; y and z neighbours are the other patch of the block in that direction (both faces), the x neighbour inside the block is given on the inner face and -1 on the outer one. `reflux_map`: Columns: the coarse patch beyond the block across the patch's outer x face (2k or 2k + 2, -1 beyond the domain), that coarse patch's face (0 lower x, 1 upper x), and the quarter 2 * (y half) + (z half) covered. Every quarter is covered by exactly one fine patch.
All inputs are finite; a program needn't handle non-finite values.
Results may differ from the reference program's by a relative error of at most 0.00005.
Values sent between devices are 32-bit elements; how exact they have to be, the bound alone decides.
A program may use at most 256 MiB of HBM per device.

```python
import jax
import jax.numpy as jnp
from jax import lax

NB = 32
NF = 5
CDEV = 2
FOLD = 10
FNEW = 14
CCAP = 3
NC = 256
NFP = 1024
N_GRP = 4
N_SFC = 32


def geometry(key):
    devices = NC // CDEV
    fine_each = 4 * CDEV
    groups = NC // 2
    centre = jax.random.randint(jax.random.fold_in(key, 11), (), 2, devices - 2)
    device_marks = jnp.arange(devices + 1, dtype=jnp.int32)
    at_ends = (device_marks == 0) | (device_marks == devices)
    shift_old = jax.random.randint(jax.random.fold_in(key, 12), (devices + 1,), -1, 2)
    shift_old = jnp.where(device_marks == centre - 1, 1, jnp.where(device_marks == centre, -1, jnp.where(device_marks == centre + 1, 1, shift_old)))
    shift_old = jnp.where(at_ends, 0, shift_old)
    shift_new = jax.random.randint(jax.random.fold_in(key, 13), (devices + 1,), -1, 2)
    shift_new = jnp.where(device_marks == centre - 1, 1, jnp.where(device_marks == centre, -2, jnp.where(device_marks == centre + 1, 2, shift_new)))
    shift_new = jnp.where(at_ends, 0, shift_new)
    bounds_old = fine_each * device_marks + shift_old
    bounds_new = bounds_old + shift_new
    patches = jnp.arange(NFP, dtype=jnp.int32)
    owner_old = jnp.sum((patches[:, None] >= bounds_old[None, 1:devices]).astype(jnp.int32), axis=1)
    owner_new = jnp.sum((patches[:, None] >= bounds_new[None, 1:devices]).astype(jnp.int32), axis=1)
    coarse_lift = jax.random.randint(jax.random.fold_in(key, 14), (devices + 1,), 0, 2)
    coarse_lift = jnp.where(device_marks == centre, 0, jnp.where(device_marks == centre + 1, 1, jnp.where(device_marks == centre + 2, 0, coarse_lift)))
    coarse_lift = jnp.where(at_ends, 0, coarse_lift)
    bounds_coarse = CDEV * device_marks + coarse_lift
    coarse_ids = jnp.arange(NC, dtype=jnp.int32)
    owner_coarse = jnp.sum((coarse_ids[:, None] >= bounds_coarse[None, 1:devices]).astype(jnp.int32), axis=1)
    orders = jax.vmap(lambda sub_key: jax.random.permutation(sub_key, 8))(jax.random.split(jax.random.fold_in(key, 15), groups)).astype(jnp.int32)
    codes = jnp.arange(8, dtype=jnp.int32)
    position = jnp.sum(codes[None, :, None] * (orders[:, :, None] == codes[None, None, :]).astype(jnp.int32), axis=1)
    child_code = orders.reshape(-1)
    group_of = patches // 8
    block_first = 8 * group_of
    x_bit = child_code % 2
    y_bit = child_code // 2 % 2
    z_bit = child_code // 4
    x_partner = block_first + position[group_of, child_code + 1 - 2 * x_bit]
    y_partner = block_first + position[group_of, child_code + 2 - 4 * y_bit]
    z_partner = block_first + position[group_of, child_code + 4 - 8 * z_bit]
    neighbours = jnp.stack([jnp.where(x_bit == 1, x_partner, -1), jnp.where(x_bit == 0, x_partner, -1), y_partner, y_partner, z_partner, z_partner], axis=1)
    target = jnp.where(x_bit == 0, 2 * group_of, jnp.where(2 * group_of + 2 < NC, 2 * group_of + 2, -1))
    face_side = jnp.where(x_bit == 0, 1, 0)
    quarter = 2 * y_bit + z_bit
    reflux = jnp.stack([target, face_side, quarter], axis=1).astype(jnp.int32)
    return (owner_coarse.astype(jnp.int32), owner_old.astype(jnp.int32), owner_new.astype(jnp.int32), neighbours.astype(jnp.int32), reflux)


def draw_coarse_owner(key, part):
    return geometry(key)[0]


def draw_fine_owner_old(key, part):
    return geometry(key)[1]


def draw_fine_owner_new(key, part):
    return geometry(key)[2]


def draw_fine_nbr(key, part):
    return geometry(key)[3]


def draw_reflux_map(key, part):
    return geometry(key)[4]


def levels(rng, extent, shards, smallest, largest):
    def one(dim, parts):
        heights = jax.random.uniform(jax.random.fold_in(jax.random.fold_in(rng, 6), dim), (parts,), jnp.float32, smallest / len(shards), largest / len(shards))
        return jnp.repeat(jnp.exp(heights), extent[dim] // parts).reshape((-1,) + (1,) * (len(extent) - dim - 1))

    gain = one(*shards[0])
    for cut in shards[1:]:
        gain = gain * one(*cut)
    return gain


def centred(key, dims, scale, bound, cuts=(), kind=jnp.bfloat16):
    level = levels(key, dims, cuts, -0.22, 0.18) if cuts else 1.0
    result = jax.random.normal(key, dims, jnp.float32) * scale * level
    return jnp.minimum(jnp.maximum(result, -bound), bound).astype(kind)


def setup_inputs(seed: int = 0) -> dict:
    streams_of = jax.random.split(jax.random.key(seed), 8)
    coarse_state = centred(streams_of[0], (N_GRP * N_SFC * CCAP, NF, NB, NB * NB), 1.0, 6.0, ((0, 128),), jnp.float32)
    fine_old = centred(streams_of[1], (N_GRP * N_SFC * FOLD, NF, NB, NB * NB), 1.0, 6.0, ((0, 128),), jnp.float32)
    coarse_owner = draw_coarse_owner(jax.random.fold_in(streams_of[7], 71), 0)
    fine_owner_old = draw_fine_owner_old(jax.random.fold_in(streams_of[7], 71), 0)
    fine_owner_new = draw_fine_owner_new(jax.random.fold_in(streams_of[7], 71), 0)
    fine_nbr = draw_fine_nbr(jax.random.fold_in(streams_of[7], 71), 0)
    reflux_map = draw_reflux_map(jax.random.fold_in(streams_of[7], 71), 0)
    return {"coarse_state": coarse_state, "fine_old": fine_old, "coarse_owner": coarse_owner, "fine_owner_old": fine_owner_old, "fine_owner_new": fine_owner_new, "fine_nbr": fine_nbr, "reflux_map": reflux_map}


background = (0.6, -0.4, 0.25)
signal = (1.8, 1.6, 1.45)
sound_sq = 1.44
courant = 0.2
opposite = (1, 0, 3, 2, 5, 4)


def face_flux(left_q, right_q, direction):
    total_q = left_q + right_q
    jump_q = right_q - left_q
    speed_a = background[direction]
    normal = total_q[1 + direction]
    pieces = [speed_a * total_q[0] + normal]
    for component in range(3):
        entry_q = speed_a * total_q[1 + component]
        if component == direction:
            entry_q = entry_q + total_q[4]
        pieces.append(entry_q)
    pieces.append(speed_a * total_q[4] + sound_sq * normal)
    return 0.5 * jnp.stack(pieces) - (0.5 * signal[direction]) * jump_q


def boundary_layers(patch_state):
    return jnp.stack([patch_state[:, 0], patch_state[:, -1], patch_state[:, :, 0], patch_state[:, :, -1], patch_state[:, :, :, 0], patch_state[:, :, :, -1]])


def advance(patch_state, ghosts):
    ext_x = jnp.concatenate([ghosts[0][:, None], patch_state, ghosts[1][:, None]], axis=1)
    flux_x = face_flux(ext_x[:, :-1], ext_x[:, 1:], 0)
    ext_y = jnp.concatenate([ghosts[2][:, :, None], patch_state, ghosts[3][:, :, None]], axis=2)
    flux_y = face_flux(ext_y[:, :, :-1], ext_y[:, :, 1:], 1)
    ext_z = jnp.concatenate([ghosts[4][:, :, :, None], patch_state, ghosts[5][:, :, :, None]], axis=3)
    flux_z = face_flux(ext_z[:, :, :, :-1], ext_z[:, :, :, 1:], 2)
    change = (flux_x[:, 1:] - flux_x[:, :-1]) + (flux_y[:, :, 1:] - flux_y[:, :, :-1]) + (flux_z[:, :, :, 1:] - flux_z[:, :, :, :-1])
    return patch_state - courant * change, flux_x[:, 0], flux_x[:, -1]


def slot_numbers(owners):
    first_index = jnp.searchsorted(owners, owners, side="left").astype(jnp.int32)
    return jnp.arange(owners.shape[0], dtype=jnp.int32) - first_index


def level_step(states, neighbours):
    layers = jax.vmap(boundary_layers)(states)
    patch_count = states.shape[0]
    face_ids = jnp.arange(6, dtype=jnp.int32)
    facing = jnp.array(opposite, dtype=jnp.int32)
    source = jnp.where(neighbours >= 0, neighbours, jnp.arange(patch_count, dtype=jnp.int32)[:, None])
    source_face = jnp.where(neighbours >= 0, facing[None, :], face_ids[None, :])
    ghosts = layers[source, source_face]
    return lax.map(lambda paired: advance(paired[0], paired[1]), (states, ghosts))


def reference(coarse_state, fine_old, coarse_owner, fine_owner_old, fine_owner_new, fine_nbr, reflux_map):
    fields = coarse_state.shape[1]
    edge_len = coarse_state.shape[2]
    half_edge = edge_len // 2
    coarse_rows = coarse_owner * CCAP + slot_numbers(coarse_owner)
    coarse = coarse_state[coarse_rows].reshape(NC, fields, edge_len, edge_len, edge_len)
    fine_rows_old = fine_owner_old * FOLD + slot_numbers(fine_owner_old)
    fine_patches = fine_old[fine_rows_old].reshape(NFP, fields, edge_len, edge_len, edge_len)
    index_c = jnp.arange(NC, dtype=jnp.int32)
    coarse_nbr = jnp.stack([jnp.where(index_c > 0, index_c - 1, -1), jnp.where(index_c < NC - 1, index_c + 1, -1), index_c, index_c, index_c, index_c], axis=1)
    coarse_new, coarse_lo, coarse_hi = level_step(coarse, coarse_nbr)
    fine_one, first_lo, first_hi = level_step(fine_patches, fine_nbr)
    fine_two, second_lo, second_hi = level_step(fine_one, fine_nbr)
    target = reflux_map[:, 0]
    face_side = reflux_map[:, 1]
    quarter = reflux_map[:, 2]
    chosen = jnp.where((face_side == 1)[:, None, None, None], first_lo + second_lo, first_hi + second_hi)
    register = chosen.reshape(NFP, fields, half_edge, 2, half_edge, 2).sum(axis=(3, 5)) * 0.125
    landing = jnp.where(target >= 0, target, NC)
    stacked = jnp.zeros((NC + 1, 2, 4, fields, half_edge, half_edge), coarse_state.dtype).at[landing, face_side, quarter].add(register)[:NC]
    covered = jnp.zeros((NC + 1, 2), coarse_state.dtype).at[landing, face_side].add(1.0)[:NC]
    covered = jnp.minimum(covered, 1.0)
    face_reg = stacked.reshape(NC, 2, 2, 2, fields, half_edge, half_edge).transpose(0, 1, 4, 2, 5, 3, 6).reshape(NC, 2, fields, edge_len, edge_len)
    coarse_new = coarse_new.at[:, :, 0].add(courant * covered[:, 0, None, None, None] * (face_reg[:, 0] - coarse_lo))
    coarse_new = coarse_new.at[:, :, -1].add(-(courant * covered[:, 1, None, None, None] * (face_reg[:, 1] - coarse_hi)))
    coarse_out = jnp.zeros_like(coarse_state).at[coarse_rows].set(coarse_new.reshape(NC, fields, edge_len, edge_len * edge_len))
    fine_rows_new = fine_owner_new * FNEW + slot_numbers(fine_owner_new)
    fine_new = jnp.zeros((N_GRP * N_SFC * FNEW, fields, edge_len, edge_len * edge_len), coarse_state.dtype).at[fine_rows_new].set(fine_two.reshape(NFP, fields, edge_len, edge_len * edge_len))
    return coarse_out, fine_new
```

```python
import functools

import jax
import jax.numpy as jnp
from jax import lax
from jax.experimental import pallas as pl
from jax.experimental.pallas import tpu as pltpu
from jax.sharding import PartitionSpec as P

MESH = pl.DeviceIdType.MESH
OLD, NEW, CAP = 10, 14, 3
PITCH = 48
background = (0.6, -0.4, 0.25)
signal = (1.8, 1.6, 1.45)
sound_sq = 1.44
courant = 0.2
TOP = 31 * 8


def weights(direction):
    up = 0.5 * courant * (signal[direction] - background[direction])
    down = 0.5 * courant * (signal[direction] + background[direction])
    return up, down


X_UP, X_DOWN = weights(0)
Y_UP, Y_DOWN = weights(1)
Z_UP, Z_DOWN = weights(2)
CENTRE = 1.0 - courant * sum(signal)
HALF = 0.5 * courant


def pick(x, idx):
    return jnp.take_along_axis(x, idx, axis=1, mode="promise_in_bounds")


def lane_ids():
    return lax.broadcasted_iota(jnp.int32, (8, 128), 1)


def step(src, s, layer, py, pz, emit):
    lane = lane_ids()
    z = lane % 32
    low, high = lane < 32, lane >= 96
    z0, z31 = z == 0, z == 31
    ghost_idx = lane // 32 + jnp.where(z31, 32, 64)
    for r in range(4):
        rows = pl.ds(8 * r, 8)

        def at(f, j, shift=0):
            return src[s, f, pl.ds(PITCH * j + 8 + 8 * r + shift, 8), :]

        for j in range(8):
            gi = ghost_idx + 4 * j

            def field(f):
                q = at(f, j)
                xm, xp = at(f, j, -1), at(f, j, 1)
                up = at(f, j + 1) if j < 7 else layer[py, f, rows, :]
                dn = at(f, j - 1) if j > 0 else layer[py, f, rows, :]
                g = pick(layer[pz, f, rows, :], gi)
                yp = pltpu.roll(jnp.where(low, up, q), 96, 1)
                ym = pltpu.roll(jnp.where(high, dn, q), 32, 1)
                zp = jnp.where(z31, g, pltpu.roll(q, 127, 1))
                zm = jnp.where(z0, g, pltpu.roll(q, 1, 1))
                lin = (
                    CENTRE * q
                    + X_UP * xp
                    + X_DOWN * xm
                    + Y_UP * yp
                    + Y_DOWN * ym
                    + Z_UP * zp
                    + Z_DOWN * zm
                )
                return lin, (xp, xm, yp, ym, zp, zm)

            lin4, (xp, xm, yp, ym, zp, zm) = field(4)
            dx, dy, dz = xp - xm, yp - ym, zp - zm
            lin, near = field(1)
            emit(r, j, 1, lin - HALF * dx)
            div = near[0] - near[1]
            lin, near = field(2)
            emit(r, j, 2, lin - HALF * dy)
            div = div + (near[2] - near[3])
            lin, near = field(3)
            emit(r, j, 3, lin - HALF * dz)
            div = div + (near[4] - near[5])
            emit(r, j, 4, lin4 - HALF * sound_sq * div)
            lin, near = field(0)
            emit(r, j, 0, lin - HALF * div)


def make_layers(src, s, layer):
    lane = lane_ids()
    slot_of = jnp.where((lane >= 32) & (lane < 96), (lane // 4) % 8, -1)
    pack_idx = 32 * (lane % 4) + jnp.where(lane >= 64, 31, 0)
    for r in range(4):
        for f in range(5):

            def at(j):
                return src[s, f, pl.ds(PITCH * j + 8 + 8 * r, 8), :]

            acc = jnp.where(lane < 64, at(0), at(7))
            for j in range(8):
                acc = jnp.where(slot_of == j, pick(at(j), pack_idx), acc)
            layer[s, f, pl.ds(8 * r, 8), :] = acc


def x_row(src, s, f, x):
    return src[s, f, pl.ds(8 + x, 8, stride=PITCH), :]


def set_x_ghost(dst, s, f, low, high):
    dst[s, f, pl.ds(7, 8, stride=PITCH), :] = low
    dst[s, f, pl.ds(40, 8, stride=PITCH), :] = high


def face_flux(left, right, direction):
    total = [left[f] + right[f] for f in range(5)]
    speed = background[direction]
    normal = total[1 + direction]
    pieces = [speed * total[0] + normal]
    for component in range(3):
        entry = speed * total[1 + component]
        if component == direction:
            entry = entry + total[4]
        pieces.append(entry)
    pieces.append(speed * total[4] + sound_sq * normal)
    return [
        0.5 * pieces[f] - 0.5 * signal[direction] * (right[f] - left[f])
        for f in range(5)
    ]


class Plan:
    def __init__(self, one, two, regs):
        self.one, self.two, self.regs = one, two, regs
        self.windows = [(1, one)] + ([(2, two)] if two else [])
        self.pool = OLD + 2 * sum(w for _, w in self.windows)
        self.reg_windows = [(k + 1, w) for k, w in enumerate(regs) if w]
        self.reg_pool = OLD + 2 * sum(w for _, w in self.reg_windows)
        self.reach = max(2 if two else 1, len(self.reg_windows))


def body_one(plan, n_grp, n_sfc, tab, fine, coarse, mig, cnew, *scr):
    q0, q1, out, c0, c1, cl, l0, l1, inbox, stage, reg, rinbox, rstage, edge, tail, tmp, dsem, ssem, rsem = scr
    devices = n_grp * n_sfc
    me = lax.axis_index("grp") * n_sfc + lax.axis_index("sfc")

    def peer(shift):
        d = lax.rem(me + shift + devices, devices)
        return (d // n_sfc, lax.rem(d, n_sfc))

    shifts = [s for k in range(1, plan.reach + 1) for s in (k, -k)]
    sems = iter(range(64))

    def send(src, dst, shift):
        k = next(sems)
        copy = pltpu.make_async_remote_copy(
            src_ref=src,
            dst_ref=dst,
            send_sem=ssem.at[k],
            recv_sem=rsem.at[k],
            device_id=peer(shift),
            device_id_type=MESH,
        )
        copy.start()
        return copy

    loads = []
    for j in range(8):
        rows, cols = pl.ds(PITCH * j + 8, 32), pl.ds(128 * j, 128)
        loads.append(
            pltpu.make_async_copy(coarse.at[:, :, :, cols], c0.at[:, :, rows, :], dsem.at[j])
        )
    for j in range(8):
        rows, cols = pl.ds(PITCH * j + 8, 32), pl.ds(128 * j, 128)
        loads.append(
            pltpu.make_async_copy(fine.at[:, :, :, cols], q0.at[:, :, rows, :], dsem.at[8 + j])
        )
    for copy in loads:
        copy.start()
    barrier = pltpu.get_barrier_semaphore()
    for shift in shifts:
        pl.semaphore_signal(barrier, inc=1, device_id=peer(shift), device_id_type=MESH)
    pl.semaphore_wait(barrier, len(shifts))
    for copy in loads[:8]:
        copy.wait()
    count, ccount = tab[40], tab[41]
    at_start, at_end = tab[42] == 1, tab[43] == 1

    for f in range(5):
        edge[0, f] = x_row(c0, jnp.maximum(ccount - 1, 0), f, 31)
        edge[1, f] = x_row(c0, 0, f, 0)
    edges = [send(edge.at[0], edge.at[2], 1), send(edge.at[1], edge.at[3], -1)]
    for copy in loads[8:]:
        copy.wait()

    def layers_of(src, layer):
        def one(s, _):
            make_layers(src, s, layer)
            inner_low = tab[30 + s] == 1
            for f in range(5):
                layer[s, f, pl.ds(32, 8), :] = jnp.where(
                    inner_low, x_row(src, s, f, 0), x_row(src, s, f, 31)
                )
            return 0

        lax.fori_loop(0, OLD, one, 0)

    def exchange(layer, part):
        copies = []
        base = 0
        off = 0
        box = inbox.at[part]
        for k, w in plan.windows:
            st = stage.at[part, pl.ds(off, w)]
            for i in range(w):
                src = jnp.maximum(count - w + i, 0)
                for f in range(5):
                    stage[part, off + i, f] = layer[src, f]
            copies.append(send(st, box.at[pl.ds(base, w)], k))
            copies.append(send(layer.at[pl.ds(0, w)], box.at[pl.ds(base + w, w)], -k))
            base += 2 * w
            off += w
        return copies

    def arrive(copies, layer, part):
        for copy in copies:
            copy.wait()

        def one(i, _):
            layer[OLD + i] = inbox[part, i]
            return 0

        lax.fori_loop(0, plan.pool - OLD, one, 0)

    def x_ghosts(src, layer):
        def one(s, _):
            inner_low = tab[30 + s] == 1
            px = tab[s]
            for f in range(5):
                other = layer[px, f, pl.ds(32, 8), :]
                low, high = x_row(src, s, f, 0), x_row(src, s, f, 31)
                set_x_ghost(
                    src,
                    s,
                    f,
                    jnp.where(inner_low, other, low),
                    jnp.where(inner_low, high, other),
                )
            return 0

        lax.fori_loop(0, OLD, one, 0)

    layers_of(q0, l0)
    ghosts = exchange(l0, 0)

    def coarse_layers(s, _):
        make_layers(c0, s, cl)
        return 0

    lax.fori_loop(0, CAP, coarse_layers, 0)
    for copy in edges:
        copy.wait()
    for c in range(CAP):
        last = ccount == c + 1
        for f in range(5):
            low = x_row(c0, c, f, 0)
            high = x_row(c0, c, f, 31)
            if c == 0:
                before = jnp.where(at_start, low, edge[2, f])
            else:
                before = x_row(c0, c - 1, f, 31)
            after = jnp.where(at_end, high, edge[3, f])
            if c < CAP - 1:
                after = jnp.where(last, after, x_row(c0, c + 1, f, 0))
            set_x_ghost(c0, c, f, before, after)

    def coarse_step(s, _):
        def emit(r, j, f, v):
            c1[s, f, pl.ds(32 * j + 8 * r, 8), :] = v

        step(c0, s, cl, s, s, emit)
        return 0

    lax.fori_loop(0, CAP, coarse_step, 0)
    arrive(ghosts, l0, 0)
    x_ghosts(q0, l0)

    def fine_one(s, _):
        def emit(r, j, f, v):
            q1[s, f, pl.ds(PITCH * j + 8 + 8 * r, 8), :] = v

        step(q0, s, l0, tab[10 + s], tab[20 + s], emit)
        return 0

    lax.fori_loop(0, OLD, fine_one, 0)
    layers_of(q1, l1)
    ghosts = exchange(l1, 1)

    lane = lane_ids()
    reg_idx = 64 * ((lane // 32) % 2) + 2 * (lane % 16)
    wide = lax.broadcasted_iota(jnp.int32, (4, 128), 1)

    def register(s, _):
        inner_low = tab[30 + s] == 1
        for f in range(5):
            v = jnp.where(
                inner_low,
                x_row(q0, s, f, 31) + x_row(q1, s, f, 31),
                x_row(q0, s, f, 0) + x_row(q1, s, f, 0),
            )
            v = v + pltpu.roll(v, 127, 1)
            v = v + pltpu.roll(v, 96, 1)
            tmp[f] = pick(v, reg_idx)
            even = tmp[f, pl.ds(0, 4, stride=2), :]
            odd = tmp[f, pl.ds(1, 4, stride=2), :]
            reg[s, pl.ds(4 * f, 4), :] = jnp.where(wide < 64, even, odd)
        reg[s, pl.ds(20, 4), :] = jnp.zeros((4, 128), jnp.float32)
        return 0

    lax.fori_loop(0, OLD, register, 0)
    regs = []
    base, off = 0, 0
    for k, w in plan.reg_windows:
        def fill(i, _):
            src = jnp.maximum(count - w + i, 0)
            rstage[off + i] = reg[src]
            return 0

        lax.fori_loop(0, w, fill, 0)
        regs.append(send(rstage.at[pl.ds(off, w)], rinbox.at[pl.ds(base, w)], k))
        regs.append(send(reg.at[pl.ds(0, w)], rinbox.at[pl.ds(base + w, w)], -k))
        base += 2 * w
        off += w
    arrive(ghosts, l1, 1)
    x_ghosts(q1, l1)

    def fine_two(s, _):
        def emit(r, j, f, v):
            out[s, f, pl.ds(8 * r, 8), pl.ds(128 * j, 128)] = v

        step(q1, s, l1, tab[10 + s], tab[20 + s], emit)
        return 0

    lax.fori_loop(0, 2, fine_two, 0)
    moves = [send(out.at[pl.ds(0, 2)], mig.at[pl.ds(12, 2)], -1)]
    lax.fori_loop(4, OLD, fine_two, 0)

    def fill_tail(f, _):
        for i in range(2):
            for r in range(4):
                tail[i, f, pl.ds(8 * r, 8), :] = out[jnp.maximum(count - 2 + i, 0), f, pl.ds(8 * r, 8), :]
        return 0

    lax.fori_loop(0, 5, fill_tail, 0)
    moves.append(send(tail, mig.at[pl.ds(10, 2)], 1))
    lax.fori_loop(2, 4, fine_two, 0)
    stores = [pltpu.make_async_copy(out, mig.at[pl.ds(0, OLD)], dsem.at[8])]
    stores[0].start()

    for copy in regs:
        copy.wait()

    def take(i, _):
        reg[OLD + i] = rinbox[i]
        return 0

    lax.fori_loop(0, plan.reg_pool - OLD, take, 0)
    right_half = (wide % 32) >= 16
    for c in range(CAP):
        for face in range(2):
            mine = [x_row(c0, c, f, 31 * face) for f in range(5)]
            ghost = [x_row(c0, c, f, 32 if face else -1) for f in range(5)]
            flux = face_flux(mine, ghost, 0) if face else face_flux(ghost, mine, 0)
            for half in range(2):
                k = 44 + c * 8 + face * 4 + half * 2
                has = jnp.where(right_half, tab[k + 1], tab[k]) >= 0
                i0, i1 = jnp.maximum(tab[k], 0), jnp.maximum(tab[k + 1], 0)
                sums = []
                for f in range(5):
                    rows = pl.ds(4 * f, 4)
                    sums.append(0.125 * jnp.where(right_half, reg[i1, rows, :], reg[i0, rows, :]))
                speed = background[0]
                value = [
                    speed * sums[0] + sums[1],
                    speed * sums[1] + sums[4],
                    speed * sums[2],
                    speed * sums[3],
                    speed * sums[4] + sound_sq * sums[1],
                ]
                for f in range(5):
                    tmp[f] = flux[f]
                    part = tmp[f, pl.ds(4 * half, 4), :]
                    rows = pl.ds(128 * half + 31 * face, 4, stride=32)
                    fix = courant * (value[f] - part)
                    fix = -fix if face else fix
                    c1[c, f, rows, :] = c1[c, f, rows, :] + jnp.where(has, fix, 0.0)
    for j in range(8):
        copy = pltpu.make_async_copy(
            c1.at[:, :, pl.ds(32 * j, 32), :], cnew.at[:, :, :, pl.ds(128 * j, 128)], dsem.at[j]
        )
        copy.start()
        stores.append(copy)
    for copy in stores:
        copy.wait()
    for copy in moves:
        copy.wait()


def body_two(tab, mig, cnew, coarse_out, fine_new, held, zeros, in_sem, out_sem):
    jobs = [(c, tab[41] > c, c, cnew, coarse_out) for c in range(CAP)]
    jobs += [(CAP + n, tab[68 + n] >= 0, tab[68 + n], mig, fine_new) for n in range(NEW)]
    for k, live, idx, src, _ in jobs:

        @pl.when(live)
        def _():
            pltpu.make_async_copy(src.at[idx], held.at[k], in_sem.at[k]).start()

    def clear(f, _):
        for r in range(4):
            zeros[f, pl.ds(8 * r, 8), :] = jnp.zeros((8, 1024), jnp.float32)
        return 0

    lax.fori_loop(0, 5, clear, 0)

    def target(k, dst):
        return dst.at[k if k < CAP else k - CAP]

    for k, live, idx, src, dst in jobs:

        @pl.when(jnp.logical_not(live))
        def _():
            pltpu.make_async_copy(zeros, target(k, dst), out_sem.at[k]).start()

    for k, live, idx, src, dst in jobs:

        @pl.when(live)
        def _():
            pltpu.make_async_copy(src.at[idx], held.at[k], in_sem.at[k]).wait()
            pltpu.make_async_copy(held.at[k], target(k, dst), out_sem.at[k]).start()

    for k, live, idx, src, dst in jobs:
        pltpu.make_async_copy(zeros, target(k, dst), out_sem.at[k]).wait()


def tables(plan, coarse_owner, owner_old, owner_new, nbr, reflux):
    me = lax.axis_index(("grp", "sfc"))
    marks = me + jnp.arange(-3, 5, dtype=jnp.int32)

    def starts(owners):
        return jnp.sum((owners[None, :] < marks[:, None]).astype(jnp.int32), axis=1)

    old, new, crs = starts(owner_old), starts(owner_new), starts(coarse_owner)
    total = owner_old.shape[0]
    ids = jnp.arange(total, dtype=jnp.int32)

    def place(p, windows):
        where = p - old[3]
        base = OLD
        for k, w in windows:
            behind = base + w - (old[4 - k] - p)
            ahead = base + w + (p - old[3 + k])
            where = jnp.where(p < old[4 - k], behind, where)
            where = jnp.where(p >= old[3 + k], ahead, where)
            base += 2 * w
        return jnp.clip(where, 0, base - 1)

    slots = jnp.arange(OLD, dtype=jnp.int32)
    mine = (ids[None, :] == old[3] + slots[:, None])[None]
    cols = jnp.stack(
        [
            jnp.maximum(nbr[:, 0], nbr[:, 1]),
            nbr[:, 2],
            nbr[:, 4],
            (nbr[:, 0] >= 0).astype(jnp.int32),
        ]
    )
    got = jnp.sum(jnp.where(mine, cols[:, None, :], 0), axis=2)
    spots = place(got[:3], plan.windows).reshape(-1)
    ccount = crs[4] - crs[3]
    key = jnp.arange(CAP * 8, dtype=jnp.int32)
    wanted = (crs[3] + key // 8) * 8 + key % 8
    code = jnp.where(reflux[:, 0] >= 0, reflux[:, 0] * 8 + reflux[:, 1] * 4 + reflux[:, 2], -1)
    spot = place(ids, plan.reg_windows) + 1
    hit = (code[None, :] == wanted[:, None]) & (key // 8 < ccount)[:, None]
    regs = jnp.sum(jnp.where(hit, spot[None, :], 0), axis=1) - 1
    n = jnp.arange(NEW, dtype=jnp.int32)
    p = new[3] + n
    src = jnp.where(
        p < old[3], OLD + 2 - (old[3] - p), jnp.where(p >= old[4], OLD + 2 + p - old[4], p - old[3])
    )
    src = jnp.where(p < new[4], jnp.clip(src, 0, OLD + 3), -1)
    misc = jnp.stack(
        [
            old[4] - old[3],
            ccount,
            (crs[3] == 0).astype(jnp.int32),
            (crs[4] == coarse_owner.shape[0]).astype(jnp.int32),
        ]
    )
    return jnp.concatenate([spots, got[3], misc, regs, src])


def stage_one(plan, n_grp, n_sfc, tab, fine, coarse):
    f32 = jnp.float32
    big = pl.BlockSpec(memory_space=pl.ANY)
    tall = 8 * PITCH
    wide_stage = plan.pool - OLD
    return pl.pallas_call(
        functools.partial(body_one, plan, n_grp, n_sfc),
        name="advance_level",
        out_shape=(
            jax.ShapeDtypeStruct((OLD + 4, 5, 32, 1024), f32),
            jax.ShapeDtypeStruct((CAP, 5, 32, 1024), f32),
        ),
        in_specs=[pl.BlockSpec(memory_space=pltpu.SMEM), big, big],
        out_specs=(big, big),
        scratch_shapes=[
            pltpu.VMEM((OLD, 5, tall, 128), f32),
            pltpu.VMEM((OLD, 5, tall, 128), f32),
            pltpu.VMEM((OLD, 5, 32, 1024), f32),
            pltpu.VMEM((CAP, 5, tall, 128), f32),
            pltpu.VMEM((CAP, 5, 256, 128), f32),
            pltpu.VMEM((CAP, 5, 32, 128), f32),
            pltpu.VMEM((plan.pool, 5, 40, 128), f32),
            pltpu.VMEM((plan.pool, 5, 40, 128), f32),
            pltpu.VMEM((2, wide_stage, 5, 40, 128), f32),
            pltpu.VMEM((2, wide_stage // 2, 5, 40, 128), f32),
            pltpu.VMEM((plan.reg_pool, 24, 128), f32),
            pltpu.VMEM((plan.reg_pool - OLD, 24, 128), f32),
            pltpu.VMEM(((plan.reg_pool - OLD) // 2, 24, 128), f32),
            pltpu.VMEM((4, 5, 8, 128), f32),
            pltpu.VMEM((2, 5, 32, 1024), f32),
            pltpu.VMEM((5, 8, 128), f32),
            pltpu.SemaphoreType.DMA((16,)),
            pltpu.SemaphoreType.DMA((24,)),
            pltpu.SemaphoreType.DMA((24,)),
        ],
        compiler_params=pltpu.CompilerParams(
            collective_id=0, has_side_effects=True, vmem_limit_bytes=58 * 2**20
        ),
    )(tab, fine, coarse)


def stage_two(tab, mig, cnew):
    f32 = jnp.float32
    big = pl.BlockSpec(memory_space=pl.ANY)
    return pl.pallas_call(
        body_two,
        name="place_patches",
        out_shape=(
            jax.ShapeDtypeStruct((CAP, 5, 32, 1024), f32),
            jax.ShapeDtypeStruct((NEW, 5, 32, 1024), f32),
        ),
        in_specs=[pl.BlockSpec(memory_space=pltpu.SMEM), big, big],
        out_specs=(big, big),
        scratch_shapes=[
            pltpu.VMEM((CAP + NEW, 5, 32, 1024), f32),
            pltpu.VMEM((5, 32, 1024), f32),
            pltpu.SemaphoreType.DMA((CAP + NEW,)),
            pltpu.SemaphoreType.DMA((CAP + NEW,)),
        ],
        compiler_params=pltpu.CompilerParams(vmem_limit_bytes=24 * 2**20),
    )(tab, mig, cnew)


def solution(mesh):
    n_grp, n_sfc = mesh.shape["grp"], mesh.shape["sfc"]
    plan = Plan(7, 1, (10, 10, 10))

    def body(coarse_state, fine_old, coarse_owner, owner_old, owner_new, nbr, reflux):
        tab = tables(plan, coarse_owner, owner_old, owner_new, nbr, reflux)
        mig, cnew = stage_one(plan, n_grp, n_sfc, tab, fine_old, coarse_state)
        return stage_two(tab, mig, cnew)

    split = P(("grp", "sfc"), None, None, None)
    return jax.shard_map(
        body,
        mesh=mesh,
        in_specs=(split, split, P(), P(), P(), P(), P()),
        out_specs=(split, split),
        check_vma=False,
    )
```

```python
import functools

import jax
import jax.numpy as jnp
from jax import lax
from jax.experimental import pallas as pl
from jax.experimental.pallas import tpu as pltpu
from jax.sharding import PartitionSpec as P

MESH = pl.DeviceIdType.MESH
OLD, NEW, CAP = 10, 14, 3
PITCH = 48
background = (0.6, -0.4, 0.25)
signal = (1.8, 1.6, 1.45)
sound_sq = 1.44
courant = 0.2
TOP = 31 * 8


def weights(direction):
    up = 0.5 * courant * (signal[direction] - background[direction])
    down = 0.5 * courant * (signal[direction] + background[direction])
    return up, down


X_UP, X_DOWN = weights(0)
Y_UP, Y_DOWN = weights(1)
Z_UP, Z_DOWN = weights(2)
CENTRE = 1.0 - courant * sum(signal)
HALF = 0.5 * courant


def pick(x, idx):
    return jnp.take_along_axis(x, idx, axis=1, mode="promise_in_bounds")


def lane_ids():
    return lax.broadcasted_iota(jnp.int32, (8, 128), 1)


def step(src, s, layer, py, pz, emit):
    lane = lane_ids()
    z = lane % 32
    low, high = lane < 32, lane >= 96
    z0, z31 = z == 0, z == 31
    ghost_idx = lane // 32 + jnp.where(z31, 32, 64)
    for r in range(4):
        rows = pl.ds(8 * r, 8)

        def at(f, j, shift=0):
            return src[s, f, pl.ds(PITCH * j + 8 + 8 * r + shift, 8), :]

        for j in range(8):
            gi = ghost_idx + 4 * j

            def field(f):
                q = at(f, j)
                xm, xp = at(f, j, -1), at(f, j, 1)
                up = at(f, j + 1) if j < 7 else layer[py, f, rows, :]
                dn = at(f, j - 1) if j > 0 else layer[py, f, rows, :]
                g = pick(layer[pz, f, rows, :], gi)
                yp = pltpu.roll(jnp.where(low, up, q), 96, 1)
                ym = pltpu.roll(jnp.where(high, dn, q), 32, 1)
                zp = jnp.where(z31, g, pltpu.roll(q, 127, 1))
                zm = jnp.where(z0, g, pltpu.roll(q, 1, 1))
                lin = (
                    CENTRE * q
                    + X_UP * xp
                    + X_DOWN * xm
                    + Y_UP * yp
                    + Y_DOWN * ym
                    + Z_UP * zp
                    + Z_DOWN * zm
                )
                return lin, (xp, xm, yp, ym, zp, zm)

            lin4, (xp, xm, yp, ym, zp, zm) = field(4)
            dx, dy, dz = xp - xm, yp - ym, zp - zm
            lin, near = field(1)
            emit(r, j, 1, lin - HALF * dx)
            div = near[0] - near[1]
            lin, near = field(2)
            emit(r, j, 2, lin - HALF * dy)
            div = div + (near[2] - near[3])
            lin, near = field(3)
            emit(r, j, 3, lin - HALF * dz)
            div = div + (near[4] - near[5])
            emit(r, j, 4, lin4 - HALF * sound_sq * div)
            lin, near = field(0)
            emit(r, j, 0, lin - HALF * div)


def make_layers(src, s, layer):
    lane = lane_ids()
    slot_of = jnp.where((lane >= 32) & (lane < 96), (lane // 4) % 8, -1)
    pack_idx = 32 * (lane % 4) + jnp.where(lane >= 64, 31, 0)
    for r in range(4):
        for f in range(5):

            def at(j):
                return src[s, f, pl.ds(PITCH * j + 8 + 8 * r, 8), :]

            acc = jnp.where(lane < 64, at(0), at(7))
            for j in range(8):
                acc = jnp.where(slot_of == j, pick(at(j), pack_idx), acc)
            layer[s, f, pl.ds(8 * r, 8), :] = acc


def x_row(src, s, f, x):
    return src[s, f, pl.ds(8 + x, 8, stride=PITCH), :]


def set_x_ghost(dst, s, f, low, high):
    dst[s, f, pl.ds(7, 8, stride=PITCH), :] = low
    dst[s, f, pl.ds(40, 8, stride=PITCH), :] = high


def face_flux(left, right, direction):
    total = [left[f] + right[f] for f in range(5)]
    speed = background[direction]
    normal = total[1 + direction]
    pieces = [speed * total[0] + normal]
    for component in range(3):
        entry = speed * total[1 + component]
        if component == direction:
            entry = entry + total[4]
        pieces.append(entry)
    pieces.append(speed * total[4] + sound_sq * normal)
    return [
        0.5 * pieces[f] - 0.5 * signal[direction] * (right[f] - left[f])
        for f in range(5)
    ]


class Plan:
    def __init__(self, one, two, regs):
        self.one, self.two, self.regs = one, two, regs
        self.windows = [(1, one), (2, two)]
        self.pool = OLD + 2 * (one + two)
        self.reg_windows = [(k + 1, w) for k, w in enumerate(regs) if w]
        self.reg_pool = OLD + 2 * sum(w for _, w in self.reg_windows)
        self.reach = max(2, len(self.reg_windows))


def body_one(
    plan, n_grp, n_sfc, own_old, own_new, own_crs, nbr, flux_map, fine, coarse, mig, cnew, tab2, *scr
):
    q0, q1, out, c0, c1, cl, l0, l1, inbox, stage, reg, rinbox, rstage, edge, tail, tmp, tab, dsem, ssem, rsem = scr
    devices = n_grp * n_sfc
    me = lax.axis_index("grp") * n_sfc + lax.axis_index("sfc")

    def peer(shift):
        d = lax.rem(me + shift + devices, devices)
        return (d // n_sfc, lax.rem(d, n_sfc))

    shifts = [s for k in range(1, plan.reach + 1) for s in (k, -k)]
    sems = iter(range(64))

    def send(src, dst, shift):
        k = next(sems)
        copy = pltpu.make_async_remote_copy(
            src_ref=src,
            dst_ref=dst,
            send_sem=ssem.at[k],
            recv_sem=rsem.at[k],
            device_id=peer(shift),
            device_id_type=MESH,
        )
        copy.start()
        return copy

    loads = []
    for j in range(8):
        rows, cols = pl.ds(PITCH * j + 8, 32), pl.ds(128 * j, 128)
        loads.append(
            pltpu.make_async_copy(coarse.at[:, :, :, cols], c0.at[:, :, rows, :], dsem.at[j])
        )
    for j in range(8):
        rows, cols = pl.ds(PITCH * j + 8, 32), pl.ds(128 * j, 128)
        loads.append(
            pltpu.make_async_copy(fine.at[:, :, :, cols], q0.at[:, :, rows, :], dsem.at[8 + j])
        )
    for copy in loads:
        copy.start()
    rest_of_tables = fill_tables(
        plan, me, own_old, own_new, own_crs, nbr, flux_map, tab, tab2
    )
    barrier = pltpu.get_barrier_semaphore()
    for shift in shifts:
        pl.semaphore_signal(barrier, inc=1, device_id=peer(shift), device_id_type=MESH)
    pl.semaphore_wait(barrier, len(shifts))
    for copy in loads[:8]:
        copy.wait()
    count, ccount = tab[40], tab[41]
    at_start, at_end = tab[42] == 1, tab[43] == 1

    for f in range(5):
        edge[0, f] = x_row(c0, jnp.clip(ccount - 1, 0, CAP - 1), f, 31)
        edge[1, f] = x_row(c0, 0, f, 0)
    edges = [send(edge.at[0], edge.at[2], 1), send(edge.at[1], edge.at[3], -1)]
    for copy in loads[8:]:
        copy.wait()

    def layers_of(src, layer):
        def one(s, _):
            make_layers(src, s, layer)
            inner_low = tab[30 + s] == 1
            for f in range(5):
                layer[s, f, pl.ds(32, 8), :] = jnp.where(
                    inner_low, x_row(src, s, f, 0), x_row(src, s, f, 31)
                )
            return 0

        lax.fori_loop(0, OLD, one, 0)

    def exchange(layer, part):
        copies = []
        base = 0
        box = inbox.at[part]
        outer = (lane_ids() < 32) | (lane_ids() >= 96)
        for k, w in plan.windows:
            for side in range(2):
                st = stage.at[part, pl.ds(base, w)]
                for i in range(w):
                    at = TO_PEER + 3 * (base + i)
                    ix, iy, iz = tab[at], tab[at + 1], tab[at + 2]
                    for f in range(5):
                        for r in range(4):
                            rows = pl.ds(8 * r, 8)
                            stage[part, base + i, f, rows, :] = jnp.where(
                                outer, layer[iy, f, rows, :], layer[iz, f, rows, :]
                            )
                        rows = pl.ds(32, 8)
                        stage[part, base + i, f, rows, :] = layer[ix, f, rows, :]
                copies.append(send(st, box.at[pl.ds(base, w)], -k if side else k))
                base += w
        return copies

    def arrive(copies, layer, part):
        for copy in copies:
            copy.wait()

        def one(i, _):
            layer[OLD + i] = inbox[part, i]
            return 0

        lax.fori_loop(0, plan.pool - OLD, one, 0)

    def x_ghosts(src, layer):
        def one(s, _):
            inner_low = tab[30 + s] == 1
            px = tab[s]
            for f in range(5):
                other = layer[px, f, pl.ds(32, 8), :]
                low, high = x_row(src, s, f, 0), x_row(src, s, f, 31)
                set_x_ghost(
                    src,
                    s,
                    f,
                    jnp.where(inner_low, other, low),
                    jnp.where(inner_low, high, other),
                )
            return 0

        lax.fori_loop(0, OLD, one, 0)

    layers_of(q0, l0)
    ghosts = exchange(l0, 0)

    rest_of_tables()
    arrive(ghosts, l0, 0)
    x_ghosts(q0, l0)

    def fine_one(s, _):
        def emit(r, j, f, v):
            q1[s, f, pl.ds(PITCH * j + 8 + 8 * r, 8), :] = v

        step(q0, s, l0, tab[10 + s], tab[20 + s], emit)
        return 0

    lax.fori_loop(0, OLD, fine_one, 0)
    layers_of(q1, l1)
    ghosts = exchange(l1, 1)

    lane = lane_ids()
    reg_idx = 64 * ((lane // 32) % 2) + 2 * (lane % 16)
    wide = lax.broadcasted_iota(jnp.int32, (4, 128), 1)

    def register(s, _):
        inner_low = tab[30 + s] == 1
        for f in range(5):
            v = jnp.where(
                inner_low,
                x_row(q0, s, f, 31) + x_row(q1, s, f, 31),
                x_row(q0, s, f, 0) + x_row(q1, s, f, 0),
            )
            v = v + pltpu.roll(v, 127, 1)
            v = v + pltpu.roll(v, 96, 1)
            tmp[f] = pick(v, reg_idx)
            even = tmp[f, pl.ds(0, 4, stride=2), :]
            odd = tmp[f, pl.ds(1, 4, stride=2), :]
            reg[s, pl.ds(4 * f, 4), :] = jnp.where(wide < 64, even, odd)
        reg[s, pl.ds(20, 4), :] = jnp.zeros((4, 128), jnp.float32)
        return 0

    lax.fori_loop(0, OLD, register, 0)
    regs = []
    base, off = 0, 0
    for k, w in plan.reg_windows:
        def fill(i, _):
            src = jnp.clip(count - w + i, 0, OLD - 1)
            rstage[off + i] = reg[src]
            return 0

        lax.fori_loop(0, w, fill, 0)
        regs.append(send(rstage.at[pl.ds(off, w)], rinbox.at[pl.ds(base, w)], k))
        regs.append(send(reg.at[pl.ds(0, w)], rinbox.at[pl.ds(base + w, w)], -k))
        base += 2 * w
        off += w
    arrive(ghosts, l1, 1)
    x_ghosts(q1, l1)

    def fine_two(s, _):
        def emit(r, j, f, v):
            out[s, f, pl.ds(8 * r, 8), pl.ds(128 * j, 128)] = v

        step(q1, s, l1, tab[10 + s], tab[20 + s], emit)
        return 0

    lax.fori_loop(0, 2, fine_two, 0)
    moves = [send(out.at[pl.ds(0, 2)], mig.at[pl.ds(12, 2)], -1)]

    def tail_two(i, _):
        s = jnp.clip(count - 2 + i, 0, OLD - 1)

        def emit(r, j, f, v):
            tail[i, f, pl.ds(8 * r, 8), pl.ds(128 * j, 128)] = v

        step(q1, s, l1, tab[10 + s], tab[20 + s], emit)
        return 0

    lax.fori_loop(0, 2, tail_two, 0)
    moves.append(send(tail, mig.at[pl.ds(10, 2)], 1))
    lax.fori_loop(2, 6, fine_two, 0)
    stores = [pltpu.make_async_copy(out.at[pl.ds(0, 6)], mig.at[pl.ds(0, 6)], dsem.at[8])]
    stores[0].start()
    lax.fori_loop(6, OLD, fine_two, 0)
    stores.append(pltpu.make_async_copy(out.at[pl.ds(6, 4)], mig.at[pl.ds(6, 4)], dsem.at[9]))
    stores[1].start()

    def coarse_layers(s, _):
        make_layers(c0, s, cl)
        return 0

    lax.fori_loop(0, CAP, coarse_layers, 0)
    for copy in edges:
        copy.wait()
    for c in range(CAP):
        last = ccount == c + 1
        for f in range(5):
            low = x_row(c0, c, f, 0)
            high = x_row(c0, c, f, 31)
            if c == 0:
                before = jnp.where(at_start, low, edge[2, f])
            else:
                before = x_row(c0, c - 1, f, 31)
            after = jnp.where(at_end, high, edge[3, f])
            if c < CAP - 1:
                after = jnp.where(last, after, x_row(c0, c + 1, f, 0))
            set_x_ghost(c0, c, f, before, after)

    def coarse_step(s, _):
        def emit(r, j, f, v):
            c1[s, f, pl.ds(32 * j + 8 * r, 8), :] = v

        step(c0, s, cl, s, s, emit)
        return 0

    lax.fori_loop(0, CAP, coarse_step, 0)
    for copy in regs:
        copy.wait()

    def take(i, _):
        reg[OLD + i] = rinbox[i]
        return 0

    lax.fori_loop(0, plan.reg_pool - OLD, take, 0)
    right_half = (wide % 32) >= 16
    for c in range(CAP):
        for face in range(2):
            mine = [x_row(c0, c, f, 31 * face) for f in range(5)]
            ghost = [x_row(c0, c, f, 32 if face else -1) for f in range(5)]
            flux = face_flux(mine, ghost, 0) if face else face_flux(ghost, mine, 0)
            for half in range(2):
                k = 44 + c * 8 + face * 4 + half * 2
                has = jnp.where(right_half, tab[k + 1], tab[k]) >= 0
                i0, i1 = jnp.maximum(tab[k], 0), jnp.maximum(tab[k + 1], 0)
                sums = []
                for f in range(5):
                    rows = pl.ds(4 * f, 4)
                    sums.append(0.125 * jnp.where(right_half, reg[i1, rows, :], reg[i0, rows, :]))
                speed = background[0]
                value = [
                    speed * sums[0] + sums[1],
                    speed * sums[1] + sums[4],
                    speed * sums[2],
                    speed * sums[3],
                    speed * sums[4] + sound_sq * sums[1],
                ]
                for f in range(5):
                    tmp[f] = flux[f]
                    part = tmp[f, pl.ds(4 * half, 4), :]
                    rows = pl.ds(128 * half + 31 * face, 4, stride=32)
                    fix = courant * (value[f] - part)
                    fix = -fix if face else fix
                    c1[c, f, rows, :] = c1[c, f, rows, :] + jnp.where(has, fix, 0.0)
    for j in range(8):
        copy = pltpu.make_async_copy(
            c1.at[:, :, pl.ds(32 * j, 32), :], cnew.at[:, :, :, pl.ds(128 * j, 128)], dsem.at[j]
        )
        copy.start()
        stores.append(copy)
    for copy in stores:
        copy.wait()
    for copy in moves:
        copy.wait()


def body_two(tab, mig, cnew, coarse_out, fine_new, held, zeros, in_sem, out_sem):
    jobs = [(c, tab[NEW] > c, c, cnew, coarse_out) for c in range(CAP)]
    jobs += [(CAP + n, tab[n] >= 0, tab[n], mig, fine_new) for n in range(NEW)]
    for k, live, idx, src, _ in jobs:

        @pl.when(live)
        def _():
            pltpu.make_async_copy(src.at[idx], held.at[k], in_sem.at[k]).start()

    def clear(f, _):
        for r in range(4):
            zeros[f, pl.ds(8 * r, 8), :] = jnp.zeros((8, 1024), jnp.float32)
        return 0

    lax.fori_loop(0, 5, clear, 0)

    def target(k, dst):
        return dst.at[k if k < CAP else k - CAP]

    for k, live, idx, src, dst in jobs:

        @pl.when(jnp.logical_not(live))
        def _():
            pltpu.make_async_copy(zeros, target(k, dst), out_sem.at[k]).start()

    for k, live, idx, src, dst in jobs:

        @pl.when(live)
        def _():
            pltpu.make_async_copy(src.at[idx], held.at[k], in_sem.at[k]).wait()
            pltpu.make_async_copy(held.at[k], target(k, dst), out_sem.at[k]).start()

    for k, live, idx, src, dst in jobs:
        pltpu.make_async_copy(zeros, target(k, dst), out_sem.at[k]).wait()


TO_PEER = 72


def fill_tables(plan, me, own_old, own_new, own_crs, nbr, flux_map, tab, tab2):
    def start(owners, mark):
        return jnp.sum((owners[...] < mark).astype(jnp.int32))

    old = [start(own_old, me + k) for k in range(-3, 5)]
    new = [start(own_new, me + k) for k in range(2)]
    crs = [start(own_crs, me + k) for k in range(2)]
    total = own_old.shape[0] * own_old.shape[1]
    base, end = old[3], old[4]
    cut, cut_end = base % 8, end % 8
    prev1, next1 = OLD, OLD + plan.one
    prev2, next2 = OLD + 2 * plan.one, OLD + 2 * plan.one + plan.two

    def patch(p):
        p = jnp.clip(p, 0, total - 1)
        return jnp.maximum(nbr[0, p], nbr[1, p]), nbr[2, p], nbr[4, p]

    def spot(p, u):
        where = u - base
        before = prev1 + jnp.where(cut <= 4, u - (base - cut), p - base)
        after = next1 + jnp.where(cut_end <= 4, p - (end - cut_end), u - end)
        where = jnp.where(u < base, before, where)
        where = jnp.where(u < old[2], prev2, where)
        where = jnp.where(u >= end, after, where)
        where = jnp.where(u >= old[5], next2, where)
        return jnp.clip(where, 0, plan.pool - 1)

    def one_patch(s, _):
        p = base + s
        nx, ny, nz = patch(p)
        tab[s] = spot(p, nx)
        tab[10 + s] = spot(p, ny)
        tab[20 + s] = spot(p, nz)
        return 0

    def one_side(s, _):
        p = base + s
        tab[30 + s] = (nbr[0, jnp.clip(p, 0, total - 1)] >= 0).astype(jnp.int32)
        return 0

    lax.fori_loop(0, OLD, one_side, 0)
    tab[40] = end - base
    tab[41] = crs[1] - crs[0]
    tab[42] = (crs[0] == 0).astype(jnp.int32)
    tab[43] = (crs[1] == 2 * own_crs.shape[1]).astype(jnp.int32)

    def local(u):
        return jnp.clip(u - base, 0, OLD - 1)

    def to_peers(i, _):
        own = local(end - cut_end + i)
        parts = patch(end + i)
        for k in range(3):
            tab[TO_PEER + 3 * i + k] = jnp.where(cut_end <= 4, own, local(parts[k]))
        parts = patch(base - cut + i)
        for k in range(3):
            at = TO_PEER + 3 * (plan.one + i) + k
            tab[at] = jnp.where(cut <= 4, local(parts[k]), local(base + i))
        return 0

    lax.fori_loop(0, plan.one, to_peers, 0)
    for i in range(plan.two):
        for k in range(3):
            at = TO_PEER + 3 * (2 * plan.one + i) + k
            tab[at] = local(end - plan.two + i)
            tab[at + 3 * plan.two] = local(base + i)

    def reg_spot(p):
        where = p - base
        at = OLD
        for k, w in plan.reg_windows:
            where = jnp.where(p < old[4 - k], at + w - (old[4 - k] - p), where)
            where = jnp.where(p >= old[3 + k], at + w + (p - old[3 + k]), where)
            at += 2 * w
        return jnp.clip(where, 0, at - 1)

    def one_face(e, _):
        c, face = e // 2, e % 2
        g = crs[0] + c
        block = (g + 1) // 2 - 1 + face
        live = g < crs[1]
        found = [jnp.int32(-1)] * 4
        for i in range(8):
            p = jnp.clip(8 * block + i, 0, total - 1)
            hit = live & (flux_map[0, p] == g) & (flux_map[1, p] == face)
            place = reg_spot(p)
            quarter = flux_map[2, p]
            for q in range(4):
                found[q] = jnp.where(hit & (quarter == q), place, found[q])
        for q in range(4):
            tab[44 + 4 * e + q] = found[q]
        return 0

    def one_row(n, _):
        p = new[0] + n
        src = p - base
        src = jnp.where(p < base, OLD + 2 - (base - p), src)
        src = jnp.where(p >= end, OLD + 2 + (p - end), src)
        tab2[n] = jnp.where(p < new[1], jnp.clip(src, 0, OLD + 3), -1)
        return 0

    def rest():
        lax.fori_loop(0, OLD, one_patch, 0)
        lax.fori_loop(0, 2 * CAP, one_face, 0)
        lax.fori_loop(0, NEW, one_row, 0)
        tab2[NEW] = crs[1] - crs[0]

    return rest


def few_cuts(coarse_owner, owner_old, reflux):
    total = owner_old.shape[0]
    ids = jnp.arange(total, dtype=jnp.int32)

    def near(k):
        edge = owner_old[0] - 1 if k < 0 else owner_old[-1] + 1
        fill = jnp.full((1,), edge, jnp.int32)
        if k < 0:
            return jnp.concatenate([fill, owner_old[:-1]])
        return jnp.concatenate([owner_old[1:], fill])

    first, last = near(-1) != owner_old, near(1) != owner_old
    cut = ids % 8
    wide = first & (cut >= 2) & (cut <= 6)
    target = reflux[:, 0]
    coarse_ids = jnp.arange(coarse_owner.shape[0], dtype=jnp.int32)
    onto = jnp.sum(
        jnp.where(coarse_ids[:, None] == target[None, :], coarse_owner[:, None], 0), axis=0
    )
    away = jnp.where(target >= 0, onto - owner_old, 0)
    far = (jnp.abs(away) > 2) | ((away == 2) & ~last) | ((away == -2) & ~first)
    return ~jnp.any(wide | far)


def stage_one(plan, number, n_grp, n_sfc, owners, nbr, flux_map, fine, coarse):
    f32 = jnp.float32
    big = pl.BlockSpec(memory_space=pl.ANY)
    smem = pl.BlockSpec(memory_space=pltpu.SMEM)
    vmem = pl.BlockSpec(memory_space=pltpu.VMEM)
    tall = 8 * PITCH
    wide_stage = plan.pool - OLD
    return pl.pallas_call(
        functools.partial(body_one, plan, n_grp, n_sfc),
        name="advance_level",
        out_shape=(
            jax.ShapeDtypeStruct((OLD + 4, 5, 32, 1024), f32),
            jax.ShapeDtypeStruct((CAP, 5, 32, 1024), f32),
            jax.ShapeDtypeStruct((16,), jnp.int32),
        ),
        in_specs=[vmem] * 3 + [smem] * 2 + [big, big],
        out_specs=(big, big, smem),
        scratch_shapes=[
            pltpu.VMEM((OLD, 5, tall, 128), f32),
            pltpu.VMEM((OLD, 5, tall, 128), f32),
            pltpu.VMEM((OLD, 5, 32, 1024), f32),
            pltpu.VMEM((CAP, 5, tall, 128), f32),
            pltpu.VMEM((CAP, 5, 256, 128), f32),
            pltpu.VMEM((CAP, 5, 32, 128), f32),
            pltpu.VMEM((plan.pool, 5, 40, 128), f32),
            pltpu.VMEM((plan.pool, 5, 40, 128), f32),
            pltpu.VMEM((2, wide_stage, 5, 40, 128), f32),
            pltpu.VMEM((2, wide_stage, 5, 40, 128), f32),
            pltpu.VMEM((plan.reg_pool, 24, 128), f32),
            pltpu.VMEM((plan.reg_pool - OLD, 24, 128), f32),
            pltpu.VMEM(((plan.reg_pool - OLD) // 2, 24, 128), f32),
            pltpu.VMEM((4, 5, 8, 128), f32),
            pltpu.VMEM((2, 5, 32, 1024), f32),
            pltpu.VMEM((5, 8, 128), f32),
            pltpu.SMEM((128,), jnp.int32),
            pltpu.SemaphoreType.DMA((16,)),
            pltpu.SemaphoreType.DMA((24,)),
            pltpu.SemaphoreType.DMA((24,)),
        ],
        compiler_params=pltpu.CompilerParams(
            collective_id=number, has_side_effects=True, vmem_limit_bytes=58 * 2**20
        ),
    )(*owners, nbr, flux_map, fine, coarse)


def stage_two(tab, mig, cnew):
    f32 = jnp.float32
    big = pl.BlockSpec(memory_space=pl.ANY)
    return pl.pallas_call(
        body_two,
        name="place_patches",
        out_shape=(
            jax.ShapeDtypeStruct((CAP, 5, 32, 1024), f32),
            jax.ShapeDtypeStruct((NEW, 5, 32, 1024), f32),
        ),
        in_specs=[pl.BlockSpec(memory_space=pltpu.SMEM), big, big],
        out_specs=(big, big),
        scratch_shapes=[
            pltpu.VMEM((CAP + NEW, 5, 32, 1024), f32),
            pltpu.VMEM((5, 32, 1024), f32),
            pltpu.SemaphoreType.DMA((CAP + NEW,)),
            pltpu.SemaphoreType.DMA((CAP + NEW,)),
        ],
        compiler_params=pltpu.CompilerParams(vmem_limit_bytes=58 * 2**20),
    )(tab, mig, cnew)


def solution(mesh):
    n_grp, n_sfc = mesh.shape["grp"], mesh.shape["sfc"]
    common, general = Plan(1, 1, (10, 1)), Plan(4, 1, (10, 10, 10))

    def body(coarse_state, fine_old, coarse_owner, owner_old, owner_new, nbr, reflux):
        owners = (owner_old.reshape(8, -1), owner_new.reshape(8, -1), coarse_owner.reshape(2, -1))
        args = (owners, nbr.T, reflux.T, fine_old, coarse_state)
        mig, cnew, tab = lax.cond(
            few_cuts(coarse_owner, owner_old, reflux),
            functools.partial(stage_one, common, 0, n_grp, n_sfc),
            functools.partial(stage_one, general, 1, n_grp, n_sfc),
            *args,
        )
        return stage_two(tab, mig, cnew)

    split = P(("grp", "sfc"), None, None, None)
    return jax.shard_map(
        body,
        mesh=mesh,
        in_specs=(split, split, P(), P(), P(), P(), P()),
        out_specs=(split, split),
        check_vma=False,
    )
```

```python
import functools

import jax
import jax.numpy as jnp
from jax import lax
from jax.experimental import pallas as pl
from jax.experimental.pallas import tpu as pltpu
from jax.sharding import PartitionSpec as P

MESH = pl.DeviceIdType.MESH
OLD, NEW, CAP = 10, 14, 3
PITCH = 48
background = (0.6, -0.4, 0.25)
signal = (1.8, 1.6, 1.45)
sound_sq = 1.44
courant = 0.2
TOP = 31 * 8


def weights(direction):
    up = 0.5 * courant * (signal[direction] - background[direction])
    down = 0.5 * courant * (signal[direction] + background[direction])
    return up, down


X_UP, X_DOWN = weights(0)
Y_UP, Y_DOWN = weights(1)
Z_UP, Z_DOWN = weights(2)
CENTRE = 1.0 - courant * sum(signal)
HALF = 0.5 * courant


def pick(x, idx):
    return jnp.take_along_axis(x, idx, axis=1, mode="promise_in_bounds")


def lane_ids():
    return lax.broadcasted_iota(jnp.int32, (8, 128), 1)


def halves(q):
    head = q.astype(jnp.bfloat16)
    rest = (q - head.astype(jnp.float32)).astype(jnp.bfloat16)
    return jnp.concatenate([head, rest], axis=1)


def set_z_shift(mat):
    row = lax.broadcasted_iota(jnp.int32, (256, 256), 0) % 128
    col = lax.broadcasted_iota(jnp.int32, (256, 256), 1)
    at = col % 128
    up = (row == at + 1) & (at % 32 != 31) & (col < 128)
    down = (row == at - 1) & (at % 32 != 0) & (col >= 128)
    mat[...] = jnp.where(up | down, 1.0, 0.0).astype(jnp.bfloat16)


def step(src, s, layer, py, pz, mat, emit):
    lane = lane_ids()
    z = lane % 32
    low, high = lane < 32, lane >= 96
    z0, z31 = z == 0, z == 31
    ghost_idx = lane // 32 + jnp.where(z31, 32, 64)
    for j in range(8):
        gi = ghost_idx + 4 * j
        whole = [halves(src[s, f, pl.ds(PITCH * j + 8, 32), :]) for f in range(5)]
        zz = jnp.dot(
            jnp.concatenate(whole, axis=0), mat[...], preferred_element_type=jnp.float32
        )
        for r in range(4):
            rows = pl.ds(8 * r, 8)

            def at(f, shift=0, jump=0):
                return src[s, f, pl.ds(PITCH * (j + jump) + 8 + 8 * r + shift, 8), :]

            def field(f):
                q = at(f)
                xm, xp = at(f, -1), at(f, 1)
                up = at(f, 0, 1) if j < 7 else layer[py, f, rows, :]
                dn = at(f, 0, -1) if j > 0 else layer[py, f, rows, :]
                g = pick(layer[pz, f, rows, :], gi)
                yp = pltpu.roll(jnp.where(low, up, q), 96, 1)
                ym = pltpu.roll(jnp.where(high, dn, q), 32, 1)
                k = 32 * f + 8 * r
                zp = jnp.where(z31, g, zz[k : k + 8, :128])
                zm = jnp.where(z0, g, zz[k : k + 8, 128:])
                lin = (
                    CENTRE * q
                    + X_UP * xp
                    + X_DOWN * xm
                    + Y_UP * yp
                    + Y_DOWN * ym
                    + Z_UP * zp
                    + Z_DOWN * zm
                )
                return lin, (xp, xm, yp, ym, zp, zm)

            lin4, (xp, xm, yp, ym, zp, zm) = field(4)
            dx, dy, dz = xp - xm, yp - ym, zp - zm
            lin, near = field(1)
            emit(r, j, 1, lin - HALF * dx)
            div = near[0] - near[1]
            lin, near = field(2)
            emit(r, j, 2, lin - HALF * dy)
            div = div + (near[2] - near[3])
            lin, near = field(3)
            emit(r, j, 3, lin - HALF * dz)
            div = div + (near[4] - near[5])
            emit(r, j, 4, lin4 - HALF * sound_sq * div)
            lin, near = field(0)
            emit(r, j, 0, lin - HALF * div)


def make_layers(src, s, layer):
    lane = lane_ids()
    slot_of = jnp.where((lane >= 32) & (lane < 96), (lane // 4) % 8, -1)
    pack_idx = 32 * (lane % 4) + jnp.where(lane >= 64, 31, 0)
    for r in range(4):
        for f in range(5):

            def at(j):
                return src[s, f, pl.ds(PITCH * j + 8 + 8 * r, 8), :]

            acc = jnp.where(lane < 64, at(0), at(7))
            for j in range(8):
                acc = jnp.where(slot_of == j, pick(at(j), pack_idx), acc)
            layer[s, f, pl.ds(8 * r, 8), :] = acc


def x_row(src, s, f, x):
    return src[s, f, pl.ds(8 + x, 8, stride=PITCH), :]


def set_x_ghost(dst, s, f, low, high):
    dst[s, f, pl.ds(7, 8, stride=PITCH), :] = low
    dst[s, f, pl.ds(40, 8, stride=PITCH), :] = high


def face_flux(left, right, direction):
    total = [left[f] + right[f] for f in range(5)]
    speed = background[direction]
    normal = total[1 + direction]
    pieces = [speed * total[0] + normal]
    for component in range(3):
        entry = speed * total[1 + component]
        if component == direction:
            entry = entry + total[4]
        pieces.append(entry)
    pieces.append(speed * total[4] + sound_sq * normal)
    return [
        0.5 * pieces[f] - 0.5 * signal[direction] * (right[f] - left[f])
        for f in range(5)
    ]


class Plan:
    def __init__(self, one, two, regs):
        self.one, self.two, self.regs = one, two, regs
        self.windows = [(1, one), (2, two)]
        self.pool = OLD + 2 * (one + two)
        self.reg_windows = [(k + 1, w) for k, w in enumerate(regs) if w]
        self.reg_pool = OLD + 2 * sum(w for _, w in self.reg_windows)
        self.reach = max(2, len(self.reg_windows))


def body_one(
    plan, n_grp, n_sfc, own_old, own_new, own_crs, nbr, flux_map, fine, coarse, mig, cnew, tab2, *scr
):
    q0, q1, out, c0, c1, cl, l0, l1, inbox, stage, reg, rinbox, rstage, edge, tail, tmp, tab, mat, dsem, ssem, rsem = scr
    devices = n_grp * n_sfc
    me = lax.axis_index("grp") * n_sfc + lax.axis_index("sfc")

    def peer(shift):
        d = lax.rem(me + shift + devices, devices)
        return (d // n_sfc, lax.rem(d, n_sfc))

    shifts = [s for k in range(1, plan.reach + 1) for s in (k, -k)]
    sems = iter(range(64))

    def send(src, dst, shift):
        k = next(sems)
        copy = pltpu.make_async_remote_copy(
            src_ref=src,
            dst_ref=dst,
            send_sem=ssem.at[k],
            recv_sem=rsem.at[k],
            device_id=peer(shift),
            device_id_type=MESH,
        )
        copy.start()
        return copy

    barrier = pltpu.get_barrier_semaphore()
    for shift in shifts:
        pl.semaphore_signal(barrier, inc=1, device_id=peer(shift), device_id_type=MESH)
    loads = []
    for src, dst, k in ((fine, q0, 0), (coarse, c0, 8)):
        for j in range(8):
            rows, cols = pl.ds(PITCH * j + 8, 32), pl.ds(128 * j, 128)
            loads.append(
                pltpu.make_async_copy(src.at[:, :, :, cols], dst.at[:, :, rows, :], dsem.at[k + j])
            )
    for copy in loads:
        copy.start()
    set_z_shift(mat)
    place_tables, late_tables = fill_tables(
        plan, me, own_old, own_new, own_crs, nbr, flux_map, tab, tab2
    )
    count, ccount = tab[40], tab[41]
    at_start, at_end = tab[42] == 1, tab[43] == 1

    def layers_of(src, layer):
        def one(s, _):
            make_layers(src, s, layer)
            inner_low = tab[30 + s] == 1
            for f in range(5):
                layer[s, f, pl.ds(32, 8), :] = jnp.where(
                    inner_low, x_row(src, s, f, 0), x_row(src, s, f, 31)
                )
            return 0

        lax.fori_loop(0, OLD, one, 0)

    def exchange(layer, part):
        copies = []
        base = 0
        box = inbox.at[part]
        outer = (lane_ids() < 32) | (lane_ids() >= 96)
        for k, w in plan.windows:
            for side in range(2):
                st = stage.at[part, pl.ds(base, w)]
                for i in range(w):
                    at = TO_PEER + 3 * (base + i)
                    ix, iy, iz = tab[at], tab[at + 1], tab[at + 2]
                    for f in range(5):
                        for r in range(4):
                            rows = pl.ds(8 * r, 8)
                            stage[part, base + i, f, rows, :] = jnp.where(
                                outer, layer[iy, f, rows, :], layer[iz, f, rows, :]
                            )
                        rows = pl.ds(32, 8)
                        stage[part, base + i, f, rows, :] = layer[ix, f, rows, :]
                copies.append(send(st, box.at[pl.ds(base, w)], -k if side else k))
                base += w
        return copies

    def arrive(copies, layer, part):
        for copy in copies:
            copy.wait()

        def one(i, _):
            layer[OLD + i] = inbox[part, i]
            return 0

        lax.fori_loop(0, plan.pool - OLD, one, 0)

    def x_ghosts(src, layer):
        def one(s, _):
            inner_low = tab[30 + s] == 1
            px = tab[s]
            for f in range(5):
                other = layer[px, f, pl.ds(32, 8), :]
                low, high = x_row(src, s, f, 0), x_row(src, s, f, 31)
                set_x_ghost(
                    src,
                    s,
                    f,
                    jnp.where(inner_low, other, low),
                    jnp.where(inner_low, high, other),
                )
            return 0

        lax.fori_loop(0, OLD, one, 0)

    for copy in loads[:8]:
        copy.wait()
    layers_of(q0, l0)
    pl.semaphore_wait(barrier, len(shifts))
    ghosts = exchange(l0, 0)
    for copy in loads[8:]:
        copy.wait()
    for f in range(5):
        edge[0, f] = x_row(c0, jnp.clip(ccount - 1, 0, CAP - 1), f, 31)
        edge[1, f] = x_row(c0, 0, f, 0)
    edges = [send(edge.at[0], edge.at[2], 1), send(edge.at[1], edge.at[3], -1)]

    place_tables()
    arrive(ghosts, l0, 0)
    x_ghosts(q0, l0)

    def fine_one(s, _):
        def emit(r, j, f, v):
            q1[s, f, pl.ds(PITCH * j + 8 + 8 * r, 8), :] = v

        step(q0, s, l0, tab[10 + s], tab[20 + s], mat, emit)
        return 0

    lax.fori_loop(0, OLD, fine_one, 0)
    layers_of(q1, l1)
    ghosts = exchange(l1, 1)

    lane = lane_ids()
    reg_idx = 64 * ((lane // 32) % 2) + 2 * (lane % 16)
    wide = lax.broadcasted_iota(jnp.int32, (4, 128), 1)

    def register(s, _):
        inner_low = tab[30 + s] == 1
        for f in range(5):
            v = jnp.where(
                inner_low,
                x_row(q0, s, f, 31) + x_row(q1, s, f, 31),
                x_row(q0, s, f, 0) + x_row(q1, s, f, 0),
            )
            v = v + pltpu.roll(v, 127, 1)
            v = v + pltpu.roll(v, 96, 1)
            tmp[f] = pick(v, reg_idx)
            even = tmp[f, pl.ds(0, 4, stride=2), :]
            odd = tmp[f, pl.ds(1, 4, stride=2), :]
            reg[s, pl.ds(4 * f, 4), :] = jnp.where(wide < 64, even, odd)
        reg[s, pl.ds(20, 4), :] = jnp.zeros((4, 128), jnp.float32)
        return 0

    lax.fori_loop(0, OLD, register, 0)
    regs = []
    base, off = 0, 0
    for k, w in plan.reg_windows:
        def fill(i, _):
            src = jnp.clip(count - w + i, 0, OLD - 1)
            rstage[off + i] = reg[src]
            return 0

        lax.fori_loop(0, w, fill, 0)
        regs.append(send(rstage.at[pl.ds(off, w)], rinbox.at[pl.ds(base, w)], k))
        regs.append(send(reg.at[pl.ds(0, w)], rinbox.at[pl.ds(base + w, w)], -k))
        base += 2 * w
        off += w
    arrive(ghosts, l1, 1)
    x_ghosts(q1, l1)

    def fine_two(s, _):
        def emit(r, j, f, v):
            out[s, f, pl.ds(8 * r, 8), pl.ds(128 * j, 128)] = v

        step(q1, s, l1, tab[10 + s], tab[20 + s], mat, emit)
        return 0

    def tail_two(i, _):
        s = jnp.clip(count - 2 + i, 0, OLD - 1)

        def emit(r, j, f, v):
            tail[i, f, pl.ds(8 * r, 8), pl.ds(128 * j, 128)] = v

        step(q1, s, l1, tab[10 + s], tab[20 + s], mat, emit)
        return 0

    moves = []
    for i in range(2):
        lax.fori_loop(i, i + 1, fine_two, 0)
        moves.append(send(out.at[pl.ds(i, 1)], mig.at[pl.ds(12 + i, 1)], -1))
        lax.fori_loop(i, i + 1, tail_two, 0)
        moves.append(send(tail.at[pl.ds(i, 1)], mig.at[pl.ds(10 + i, 1)], 1))
    late_tables()
    lax.fori_loop(2, 6, fine_two, 0)
    stores = [pltpu.make_async_copy(out.at[pl.ds(0, 6)], mig.at[pl.ds(0, 6)], dsem.at[8])]
    stores[0].start()
    lax.fori_loop(6, OLD, fine_two, 0)
    stores.append(pltpu.make_async_copy(out.at[pl.ds(6, 4)], mig.at[pl.ds(6, 4)], dsem.at[9]))
    stores[1].start()

    def coarse_layers(s, _):
        make_layers(c0, s, cl)
        return 0

    lax.fori_loop(0, CAP, coarse_layers, 0)
    for copy in edges:
        copy.wait()
    for c in range(CAP):
        last = ccount == c + 1
        for f in range(5):
            low = x_row(c0, c, f, 0)
            high = x_row(c0, c, f, 31)
            if c == 0:
                before = jnp.where(at_start, low, edge[2, f])
            else:
                before = x_row(c0, c - 1, f, 31)
            after = jnp.where(at_end, high, edge[3, f])
            if c < CAP - 1:
                after = jnp.where(last, after, x_row(c0, c + 1, f, 0))
            set_x_ghost(c0, c, f, before, after)

    def coarse_step(s, _):
        def emit(r, j, f, v):
            c1[s, f, pl.ds(32 * j + 8 * r, 8), :] = v

        step(c0, s, cl, s, s, mat, emit)
        return 0

    lax.fori_loop(0, CAP, coarse_step, 0)
    for copy in regs:
        copy.wait()

    def take(i, _):
        reg[OLD + i] = rinbox[i]
        return 0

    lax.fori_loop(0, plan.reg_pool - OLD, take, 0)
    right_half = (wide % 32) >= 16
    for c in range(CAP):
        for face in range(2):
            mine = [x_row(c0, c, f, 31 * face) for f in range(5)]
            ghost = [x_row(c0, c, f, 32 if face else -1) for f in range(5)]
            flux = face_flux(mine, ghost, 0) if face else face_flux(ghost, mine, 0)
            for half in range(2):
                k = 44 + c * 8 + face * 4 + half * 2
                has = jnp.where(right_half, tab[k + 1], tab[k]) >= 0
                i0, i1 = jnp.maximum(tab[k], 0), jnp.maximum(tab[k + 1], 0)
                sums = []
                for f in range(5):
                    rows = pl.ds(4 * f, 4)
                    sums.append(0.125 * jnp.where(right_half, reg[i1, rows, :], reg[i0, rows, :]))
                speed = background[0]
                value = [
                    speed * sums[0] + sums[1],
                    speed * sums[1] + sums[4],
                    speed * sums[2],
                    speed * sums[3],
                    speed * sums[4] + sound_sq * sums[1],
                ]
                for f in range(5):
                    tmp[f] = flux[f]
                    part = tmp[f, pl.ds(4 * half, 4), :]
                    rows = pl.ds(128 * half + 31 * face, 4, stride=32)
                    fix = courant * (value[f] - part)
                    fix = -fix if face else fix
                    c1[c, f, rows, :] = c1[c, f, rows, :] + jnp.where(has, fix, 0.0)
    for j in range(8):
        copy = pltpu.make_async_copy(
            c1.at[:, :, pl.ds(32 * j, 32), :], cnew.at[:, :, :, pl.ds(128 * j, 128)], dsem.at[j]
        )
        copy.start()
        stores.append(copy)
    for copy in stores:
        copy.wait()
    for copy in moves:
        copy.wait()


def body_two(tab, mig, cnew, coarse_out, fine_new, held, zeros, in_sem, out_sem):
    jobs = [(c, tab[NEW] > c, c, cnew, coarse_out) for c in range(CAP)]
    jobs += [(CAP + n, tab[n] >= 0, tab[n], mig, fine_new) for n in range(NEW)]
    for k, live, idx, src, _ in jobs:

        @pl.when(live)
        def _():
            pltpu.make_async_copy(src.at[idx], held.at[k], in_sem.at[k]).start()

    def clear(f, _):
        for r in range(4):
            zeros[f, pl.ds(8 * r, 8), :] = jnp.zeros((8, 1024), jnp.float32)
        return 0

    lax.fori_loop(0, 5, clear, 0)

    def target(k, dst):
        return dst.at[k if k < CAP else k - CAP]

    for k, live, idx, src, dst in jobs:

        @pl.when(jnp.logical_not(live))
        def _():
            pltpu.make_async_copy(zeros, target(k, dst), out_sem.at[k]).start()

    for k, live, idx, src, dst in jobs:

        @pl.when(live)
        def _():
            pltpu.make_async_copy(src.at[idx], held.at[k], in_sem.at[k]).wait()
            pltpu.make_async_copy(held.at[k], target(k, dst), out_sem.at[k]).start()

    for k, live, idx, src, dst in jobs:
        pltpu.make_async_copy(zeros, target(k, dst), out_sem.at[k]).wait()


TO_PEER = 72


def fill_tables(plan, me, own_old, own_new, own_crs, nbr, flux_map, tab, tab2):
    def start(owners, mark):
        return jnp.sum((owners[...] < mark).astype(jnp.int32))

    old = [start(own_old, me + k) for k in range(-3, 5)]
    new = [start(own_new, me + k) for k in range(2)]
    crs = [start(own_crs, me + k) for k in range(2)]
    total = own_old.shape[0] * own_old.shape[1]
    base, end = old[3], old[4]
    cut, cut_end = base % 8, end % 8
    prev1, next1 = OLD, OLD + plan.one
    prev2, next2 = OLD + 2 * plan.one, OLD + 2 * plan.one + plan.two

    def patch(p):
        p = jnp.clip(p, 0, total - 1)
        return jnp.maximum(nbr[0, p], nbr[1, p]), nbr[2, p], nbr[4, p]

    def spot(p, u):
        where = u - base
        before = prev1 + jnp.where(cut <= 4, u - (base - cut), p - base)
        after = next1 + jnp.where(cut_end <= 4, p - (end - cut_end), u - end)
        where = jnp.where(u < base, before, where)
        where = jnp.where(u < old[2], prev2, where)
        where = jnp.where(u >= end, after, where)
        where = jnp.where(u >= old[5], next2, where)
        return jnp.clip(where, 0, plan.pool - 1)

    def one_patch(s, _):
        p = base + s
        nx, ny, nz = patch(p)
        tab[s] = spot(p, nx)
        tab[10 + s] = spot(p, ny)
        tab[20 + s] = spot(p, nz)
        return 0

    def one_side(s, _):
        p = base + s
        tab[30 + s] = (nbr[0, jnp.clip(p, 0, total - 1)] >= 0).astype(jnp.int32)
        return 0

    lax.fori_loop(0, OLD, one_side, 0)
    tab[40] = end - base
    tab[41] = crs[1] - crs[0]
    tab[42] = (crs[0] == 0).astype(jnp.int32)
    tab[43] = (crs[1] == 2 * own_crs.shape[1]).astype(jnp.int32)

    def local(u):
        return jnp.clip(u - base, 0, OLD - 1)

    def to_peers(i, _):
        own = local(end - cut_end + i)
        parts = patch(end + i)
        for k in range(3):
            tab[TO_PEER + 3 * i + k] = jnp.where(cut_end <= 4, own, local(parts[k]))
        parts = patch(base - cut + i)
        for k in range(3):
            at = TO_PEER + 3 * (plan.one + i) + k
            tab[at] = jnp.where(cut <= 4, local(parts[k]), local(base + i))
        return 0

    lax.fori_loop(0, plan.one, to_peers, 0)
    for i in range(plan.two):
        for k in range(3):
            at = TO_PEER + 3 * (2 * plan.one + i) + k
            tab[at] = local(end - plan.two + i)
            tab[at + 3 * plan.two] = local(base + i)

    def reg_spot(p):
        where = p - base
        at = OLD
        for k, w in plan.reg_windows:
            where = jnp.where(p < old[4 - k], at + w - (old[4 - k] - p), where)
            where = jnp.where(p >= old[3 + k], at + w + (p - old[3 + k]), where)
            at += 2 * w
        return jnp.clip(where, 0, at - 1)

    def one_face(e, _):
        c, face = e // 2, e % 2
        g = crs[0] + c
        block = (g + 1) // 2 - 1 + face
        live = g < crs[1]
        found = [jnp.int32(-1)] * 4
        for i in range(8):
            p = jnp.clip(8 * block + i, 0, total - 1)
            hit = live & (flux_map[0, p] == g) & (flux_map[1, p] == face)
            place = reg_spot(p)
            quarter = flux_map[2, p]
            for q in range(4):
                found[q] = jnp.where(hit & (quarter == q), place, found[q])
        for q in range(4):
            tab[44 + 4 * e + q] = found[q]
        return 0

    def one_row(n, _):
        p = new[0] + n
        src = p - base
        src = jnp.where(p < base, OLD + 2 - (base - p), src)
        src = jnp.where(p >= end, OLD + 2 + (p - end), src)
        tab2[n] = jnp.where(p < new[1], jnp.clip(src, 0, OLD + 3), -1)
        return 0

    def place():
        lax.fori_loop(0, OLD, one_patch, 0)

    def late():
        lax.fori_loop(0, 2 * CAP, one_face, 0)
        lax.fori_loop(0, NEW, one_row, 0)
        tab2[NEW] = crs[1] - crs[0]

    return place, late


def cuts_body(own_old, own_crs, flux_map, wide_out, target_rows):
    owner = own_old[...]
    lane = lane_ids()
    for j in range(8):
        target_rows[pl.ds(j, 1), :] = flux_map[pl.ds(0, 1), pl.ds(128 * j, 128)]
    target = target_rows[...]

    def moved(lane_shift, row_shift, edge):
        turned = pltpu.roll(owner, lane_shift, 1)
        return jnp.where(lane == edge, pltpu.roll(turned, row_shift, 0), turned)

    first, last = moved(1, 1, 0) != owner, moved(127, 7, 127) != owner
    cut = lane % 8
    wide = first & (cut >= 2) & (cut <= 6)
    spot = jnp.maximum(target, 0) % 128
    onto = [pick(jnp.broadcast_to(own_crs[pl.ds(k, 1), :], (8, 128)), spot) for k in range(2)]
    away = jnp.where(target >= 0, jnp.where(target < 128, onto[0], onto[1]) - owner, 0)
    far = (jnp.abs(away) > 2) | ((away == 2) & ~last) | ((away == -2) & ~first)
    wide_out[0] = jnp.max(jnp.where(wide | far, 1, 0))


def cuts(owners, flux_map):
    vmem = pl.BlockSpec(memory_space=pltpu.VMEM)
    return pl.pallas_call(
        cuts_body,
        name="cuts",
        out_shape=jax.ShapeDtypeStruct((1,), jnp.int32),
        in_specs=[vmem] * 3,
        out_specs=pl.BlockSpec(memory_space=pltpu.SMEM),
        scratch_shapes=[pltpu.VMEM((8, 128), jnp.int32)],
    )(owners[0], owners[2], flux_map)


def stage_one(plan, number, n_grp, n_sfc, owners, nbr, flux_map, fine, coarse):
    f32 = jnp.float32
    big = pl.BlockSpec(memory_space=pl.ANY)
    smem = pl.BlockSpec(memory_space=pltpu.SMEM)
    vmem = pl.BlockSpec(memory_space=pltpu.VMEM)
    tall = 8 * PITCH
    wide_stage = plan.pool - OLD
    return pl.pallas_call(
        functools.partial(body_one, plan, n_grp, n_sfc),
        name="advance_level",
        out_shape=(
            jax.ShapeDtypeStruct((OLD + 4, 5, 32, 1024), f32),
            jax.ShapeDtypeStruct((CAP, 5, 32, 1024), f32),
            jax.ShapeDtypeStruct((16,), jnp.int32),
        ),
        in_specs=[vmem] * 3 + [smem] * 2 + [big, big],
        out_specs=(big, big, smem),
        scratch_shapes=[
            pltpu.VMEM((OLD, 5, tall, 128), f32),
            pltpu.VMEM((OLD, 5, tall, 128), f32),
            pltpu.VMEM((OLD, 5, 32, 1024), f32),
            pltpu.VMEM((CAP, 5, tall, 128), f32),
            pltpu.VMEM((CAP, 5, 256, 128), f32),
            pltpu.VMEM((CAP, 5, 32, 128), f32),
            pltpu.VMEM((plan.pool, 5, 40, 128), f32),
            pltpu.VMEM((plan.pool, 5, 40, 128), f32),
            pltpu.VMEM((2, wide_stage, 5, 40, 128), f32),
            pltpu.VMEM((2, wide_stage, 5, 40, 128), f32),
            pltpu.VMEM((plan.reg_pool, 24, 128), f32),
            pltpu.VMEM((plan.reg_pool - OLD, 24, 128), f32),
            pltpu.VMEM(((plan.reg_pool - OLD) // 2, 24, 128), f32),
            pltpu.VMEM((4, 5, 8, 128), f32),
            pltpu.VMEM((2, 5, 32, 1024), f32),
            pltpu.VMEM((5, 8, 128), f32),
            pltpu.SMEM((128,), jnp.int32),
            pltpu.VMEM((256, 256), jnp.bfloat16),
            pltpu.SemaphoreType.DMA((16,)),
            pltpu.SemaphoreType.DMA((24,)),
            pltpu.SemaphoreType.DMA((24,)),
        ],
        compiler_params=pltpu.CompilerParams(
            collective_id=number, has_side_effects=True, vmem_limit_bytes=58 * 2**20
        ),
    )(*owners, nbr, flux_map, fine, coarse)


def stage_two(tab, mig, cnew):
    f32 = jnp.float32
    big = pl.BlockSpec(memory_space=pl.ANY)
    return pl.pallas_call(
        body_two,
        name="place_patches",
        out_shape=(
            jax.ShapeDtypeStruct((CAP, 5, 32, 1024), f32),
            jax.ShapeDtypeStruct((NEW, 5, 32, 1024), f32),
        ),
        in_specs=[pl.BlockSpec(memory_space=pltpu.SMEM), big, big],
        out_specs=(big, big),
        scratch_shapes=[
            pltpu.VMEM((CAP + NEW, 5, 32, 1024), f32),
            pltpu.VMEM((5, 32, 1024), f32),
            pltpu.SemaphoreType.DMA((CAP + NEW,)),
            pltpu.SemaphoreType.DMA((CAP + NEW,)),
        ],
        compiler_params=pltpu.CompilerParams(vmem_limit_bytes=58 * 2**20),
    )(tab, mig, cnew)


def solution(mesh):
    n_grp, n_sfc = mesh.shape["grp"], mesh.shape["sfc"]
    common, general = Plan(1, 1, (10, 1)), Plan(4, 1, (10, 10, 10))

    def body(coarse_state, fine_old, coarse_owner, owner_old, owner_new, nbr, reflux):
        owners = (owner_old.reshape(8, -1), owner_new.reshape(8, -1), coarse_owner.reshape(2, -1))
        args = (owners, nbr.T, reflux.T, fine_old, coarse_state)
        mig, cnew, tab = lax.cond(
            cuts(owners, reflux.T)[0] == 0,
            functools.partial(stage_one, common, 0, n_grp, n_sfc),
            functools.partial(stage_one, general, 1, n_grp, n_sfc),
            *args,
        )
        return stage_two(tab, mig, cnew)

    split = P(("grp", "sfc"), None, None, None)
    return jax.shard_map(
        body,
        mesh=mesh,
        in_specs=(split, split, P(), P(), P(), P(), P()),
        out_specs=(split, split),
        check_vma=False,
    )
```

```python
import functools

import jax
import jax.numpy as jnp
from jax import lax
from jax.experimental import pallas as pl
from jax.experimental.pallas import tpu as pltpu
from jax.sharding import PartitionSpec as P

MESH = pl.DeviceIdType.MESH
OLD, NEW, CAP = 10, 14, 3
PITCH = 48
background = (0.6, -0.4, 0.25)
signal = (1.8, 1.6, 1.45)
sound_sq = 1.44
courant = 0.2
TOP = 31 * 8


def weights(direction):
    up = 0.5 * courant * (signal[direction] - background[direction])
    down = 0.5 * courant * (signal[direction] + background[direction])
    return up, down


X_UP, X_DOWN = weights(0)
Y_UP, Y_DOWN = weights(1)
Z_UP, Z_DOWN = weights(2)
CENTRE = 1.0 - courant * sum(signal)
HALF = 0.5 * courant


def pick(x, idx):
    return jnp.take_along_axis(x, idx, axis=1, mode="promise_in_bounds")


def lane_ids():
    return lax.broadcasted_iota(jnp.int32, (8, 128), 1)


def halves(q):
    head = q.astype(jnp.bfloat16)
    rest = (q - head.astype(jnp.float32)).astype(jnp.bfloat16)
    return jnp.concatenate([head, rest], axis=1)


def set_z_shift(mat):
    row = lax.broadcasted_iota(jnp.int32, (256, 256), 0) % 128
    col = lax.broadcasted_iota(jnp.int32, (256, 256), 1)
    at = col % 128
    up = (row == at + 1) & (at % 32 != 31) & (col < 128)
    down = (row == at - 1) & (at % 32 != 0) & (col >= 128)
    mat[...] = jnp.where(up | down, 1.0, 0.0).astype(jnp.bfloat16)


def step(src, s, layer, py, pz, mat, emit):
    lane = lane_ids()
    z = lane % 32
    low, high = lane < 32, lane >= 96
    z0, z31 = z == 0, z == 31
    ghost_idx = lane // 32 + jnp.where(z31, 32, 64)
    for j in range(8):
        gi = ghost_idx + 4 * j
        whole = [halves(src[s, f, pl.ds(PITCH * j + 8, 32), :]) for f in range(5)]
        zz = jnp.dot(
            jnp.concatenate(whole, axis=0), mat[...], preferred_element_type=jnp.float32
        )
        for r in range(4):
            rows = pl.ds(8 * r, 8)

            def at(f, shift=0, jump=0):
                return src[s, f, pl.ds(PITCH * (j + jump) + 8 + 8 * r + shift, 8), :]

            def field(f):
                q = at(f)
                xm, xp = at(f, -1), at(f, 1)
                up = at(f, 0, 1) if j < 7 else layer[py, f, rows, :]
                dn = at(f, 0, -1) if j > 0 else layer[py, f, rows, :]
                g = pick(layer[pz, f, rows, :], gi)
                yp = pltpu.roll(jnp.where(low, up, q), 96, 1)
                ym = pltpu.roll(jnp.where(high, dn, q), 32, 1)
                k = 32 * f + 8 * r
                zp = jnp.where(z31, g, zz[k : k + 8, :128])
                zm = jnp.where(z0, g, zz[k : k + 8, 128:])
                lin = (
                    CENTRE * q
                    + X_UP * xp
                    + X_DOWN * xm
                    + Y_UP * yp
                    + Y_DOWN * ym
                    + Z_UP * zp
                    + Z_DOWN * zm
                )
                return lin, (xp, xm, yp, ym, zp, zm)

            lin4, (xp, xm, yp, ym, zp, zm) = field(4)
            dx, dy, dz = xp - xm, yp - ym, zp - zm
            lin, near = field(1)
            emit(r, j, 1, lin - HALF * dx)
            div = near[0] - near[1]
            lin, near = field(2)
            emit(r, j, 2, lin - HALF * dy)
            div = div + (near[2] - near[3])
            lin, near = field(3)
            emit(r, j, 3, lin - HALF * dz)
            div = div + (near[4] - near[5])
            emit(r, j, 4, lin4 - HALF * sound_sq * div)
            lin, near = field(0)
            emit(r, j, 0, lin - HALF * div)


def make_layers(src, s, layer):
    lane = lane_ids()
    slot_of = jnp.where((lane >= 32) & (lane < 96), (lane // 4) % 8, -1)
    pack_idx = 32 * (lane % 4) + jnp.where(lane >= 64, 31, 0)
    for r in range(4):
        for f in range(5):

            def at(j):
                return src[s, f, pl.ds(PITCH * j + 8 + 8 * r, 8), :]

            acc = jnp.where(lane < 64, at(0), at(7))
            for j in range(8):
                acc = jnp.where(slot_of == j, pick(at(j), pack_idx), acc)
            layer[s, f, pl.ds(8 * r, 8), :] = acc


def x_row(src, s, f, x):
    return src[s, f, pl.ds(8 + x, 8, stride=PITCH), :]


def set_x_ghost(dst, s, f, low, high):
    dst[s, f, pl.ds(7, 8, stride=PITCH), :] = low
    dst[s, f, pl.ds(40, 8, stride=PITCH), :] = high


def face_flux(left, right, direction):
    total = [left[f] + right[f] for f in range(5)]
    speed = background[direction]
    normal = total[1 + direction]
    pieces = [speed * total[0] + normal]
    for component in range(3):
        entry = speed * total[1 + component]
        if component == direction:
            entry = entry + total[4]
        pieces.append(entry)
    pieces.append(speed * total[4] + sound_sq * normal)
    return [
        0.5 * pieces[f] - 0.5 * signal[direction] * (right[f] - left[f])
        for f in range(5)
    ]


class Plan:
    def __init__(self, one, two, regs):
        self.one, self.two, self.regs = one, two, regs
        self.windows = [(1, one), (2, two)]
        self.pool = OLD + 2 * (one + two)
        self.reg_windows = [(k + 1, w) for k, w in enumerate(regs) if w]
        self.reg_pool = OLD + 2 * sum(w for _, w in self.reg_windows)
        self.reach = max(2, len(self.reg_windows))


def body_one(
    plan, n_grp, n_sfc, own_old, own_new, own_crs, nbr, flux_map, fine, coarse, mig, cnew, tab2, *scr
):
    q0, q1, out, c0, c1, cl, l0, l1, inbox, stage, reg, rinbox, rstage, edge, tail, tmp, tab, mat, dsem, ssem, rsem = scr
    devices = n_grp * n_sfc
    me = lax.axis_index("grp") * n_sfc + lax.axis_index("sfc")

    def peer(shift):
        d = lax.rem(me + shift + devices, devices)
        return (d // n_sfc, lax.rem(d, n_sfc))

    shifts = [s for k in range(1, plan.reach + 1) for s in (k, -k)]
    sems = iter(range(64))

    def send(src, dst, shift):
        k = next(sems)
        copy = pltpu.make_async_remote_copy(
            src_ref=src,
            dst_ref=dst,
            send_sem=ssem.at[k],
            recv_sem=rsem.at[k],
            device_id=peer(shift),
            device_id_type=MESH,
        )
        copy.start()
        return copy

    barrier = pltpu.get_barrier_semaphore()
    for shift in shifts:
        pl.semaphore_signal(barrier, inc=1, device_id=peer(shift), device_id_type=MESH)
    loads = []
    for src, dst, k, first, n in ((fine, q0, 0, 0, 3), (fine, q0, 8, 3, 7), (coarse, c0, 16, 0, CAP)):
        for j in range(8):
            rows, cols = pl.ds(PITCH * j + 8, 32), pl.ds(128 * j, 128)
            some = pl.ds(first, n)
            loads.append(
                pltpu.make_async_copy(
                    src.at[some, :, :, cols], dst.at[some, :, rows, :], dsem.at[k + j]
                )
            )
    for copy in loads:
        copy.start()
    set_z_shift(mat)
    place_tables, late_tables = fill_tables(
        plan, me, own_old, own_new, own_crs, nbr, flux_map, tab, tab2
    )
    count, ccount = tab[40], tab[41]
    at_start, at_end = tab[42] == 1, tab[43] == 1

    def layers_of(src, layer, first=0, end=OLD):
        def one(s, _):
            make_layers(src, s, layer)
            inner_low = tab[30 + s] == 1
            for f in range(5):
                layer[s, f, pl.ds(32, 8), :] = jnp.where(
                    inner_low, x_row(src, s, f, 0), x_row(src, s, f, 31)
                )
            return 0

        lax.fori_loop(first, end, one, 0)

    def exchange(layer, part):
        copies = []
        base = 0
        box = inbox.at[part]
        outer = (lane_ids() < 32) | (lane_ids() >= 96)
        for k, w in plan.windows:
            for side in range(2):
                st = stage.at[part, pl.ds(base, w)]
                for i in range(w):
                    at = TO_PEER + 3 * (base + i)
                    ix, iy, iz = tab[at], tab[at + 1], tab[at + 2]
                    for f in range(5):
                        for r in range(4):
                            rows = pl.ds(8 * r, 8)
                            stage[part, base + i, f, rows, :] = jnp.where(
                                outer, layer[iy, f, rows, :], layer[iz, f, rows, :]
                            )
                        rows = pl.ds(32, 8)
                        stage[part, base + i, f, rows, :] = layer[ix, f, rows, :]
                copies.append(send(st, box.at[pl.ds(base, w)], -k if side else k))
                base += w
        return copies

    def arrive(copies, layer, part):
        for copy in copies:
            copy.wait()

        def one(i, _):
            layer[OLD + i] = inbox[part, i]
            return 0

        lax.fori_loop(0, plan.pool - OLD, one, 0)

    def x_ghosts(src, layer):
        def one(s, _):
            inner_low = tab[30 + s] == 1
            px = tab[s]
            for f in range(5):
                other = layer[px, f, pl.ds(32, 8), :]
                low, high = x_row(src, s, f, 0), x_row(src, s, f, 31)
                set_x_ghost(
                    src,
                    s,
                    f,
                    jnp.where(inner_low, other, low),
                    jnp.where(inner_low, high, other),
                )
            return 0

        lax.fori_loop(0, OLD, one, 0)

    for copy in loads[:8]:
        copy.wait()
    layers_of(q0, l0, 0, 3)
    for copy in loads[8:16]:
        copy.wait()
    layers_of(q0, l0, 3, OLD)
    pl.semaphore_wait(barrier, len(shifts))
    ghosts = exchange(l0, 0)
    for copy in loads[16:]:
        copy.wait()
    for f in range(5):
        edge[0, f] = x_row(c0, jnp.clip(ccount - 1, 0, CAP - 1), f, 31)
        edge[1, f] = x_row(c0, 0, f, 0)
    edges = [send(edge.at[0], edge.at[2], 1), send(edge.at[1], edge.at[3], -1)]

    place_tables()
    arrive(ghosts, l0, 0)
    x_ghosts(q0, l0)

    def fine_one(s, _):
        def emit(r, j, f, v):
            q1[s, f, pl.ds(PITCH * j + 8 + 8 * r, 8), :] = v

        step(q0, s, l0, tab[10 + s], tab[20 + s], mat, emit)
        return 0

    lax.fori_loop(0, OLD, fine_one, 0)
    layers_of(q1, l1)
    ghosts = exchange(l1, 1)

    lane = lane_ids()
    reg_idx = 64 * ((lane // 32) % 2) + 2 * (lane % 16)
    wide = lax.broadcasted_iota(jnp.int32, (4, 128), 1)

    def register(s, _):
        inner_low = tab[30 + s] == 1
        for f in range(5):
            v = jnp.where(
                inner_low,
                x_row(q0, s, f, 31) + x_row(q1, s, f, 31),
                x_row(q0, s, f, 0) + x_row(q1, s, f, 0),
            )
            v = v + pltpu.roll(v, 127, 1)
            v = v + pltpu.roll(v, 96, 1)
            tmp[f] = pick(v, reg_idx)
            even = tmp[f, pl.ds(0, 4, stride=2), :]
            odd = tmp[f, pl.ds(1, 4, stride=2), :]
            reg[s, pl.ds(4 * f, 4), :] = jnp.where(wide < 64, even, odd)
        reg[s, pl.ds(20, 4), :] = jnp.zeros((4, 128), jnp.float32)
        return 0

    lax.fori_loop(0, OLD, register, 0)
    regs = []
    base, off = 0, 0
    for k, w in plan.reg_windows:
        def fill(i, _):
            src = jnp.clip(count - w + i, 0, OLD - 1)
            rstage[off + i] = reg[src]
            return 0

        lax.fori_loop(0, w, fill, 0)
        regs.append(send(rstage.at[pl.ds(off, w)], rinbox.at[pl.ds(base, w)], k))
        regs.append(send(reg.at[pl.ds(0, w)], rinbox.at[pl.ds(base + w, w)], -k))
        base += 2 * w
        off += w
    arrive(ghosts, l1, 1)
    x_ghosts(q1, l1)

    def fine_two(s, _):
        def emit(r, j, f, v):
            out[s, f, pl.ds(8 * r, 8), pl.ds(128 * j, 128)] = v

        step(q1, s, l1, tab[10 + s], tab[20 + s], mat, emit)
        return 0

    def tail_two(i, _):
        s = jnp.clip(count - 2 + i, 0, OLD - 1)

        def emit(r, j, f, v):
            tail[i, f, pl.ds(8 * r, 8), pl.ds(128 * j, 128)] = v

        step(q1, s, l1, tab[10 + s], tab[20 + s], mat, emit)
        return 0

    moves = []
    for i in range(2):
        lax.fori_loop(i, i + 1, fine_two, 0)
        moves.append(send(out.at[pl.ds(i, 1)], mig.at[pl.ds(12 + i, 1)], -1))
        lax.fori_loop(i, i + 1, tail_two, 0)
        moves.append(send(tail.at[pl.ds(i, 1)], mig.at[pl.ds(10 + i, 1)], 1))
    late_tables()
    lax.fori_loop(2, 6, fine_two, 0)
    stores = [pltpu.make_async_copy(out.at[pl.ds(0, 6)], mig.at[pl.ds(0, 6)], dsem.at[8])]
    stores[0].start()
    lax.fori_loop(6, OLD, fine_two, 0)
    stores.append(pltpu.make_async_copy(out.at[pl.ds(6, 4)], mig.at[pl.ds(6, 4)], dsem.at[9]))
    stores[1].start()

    def coarse_layers(s, _):
        make_layers(c0, s, cl)
        return 0

    lax.fori_loop(0, CAP, coarse_layers, 0)
    for copy in edges:
        copy.wait()
    for c in range(CAP):
        last = ccount == c + 1
        for f in range(5):
            low = x_row(c0, c, f, 0)
            high = x_row(c0, c, f, 31)
            if c == 0:
                before = jnp.where(at_start, low, edge[2, f])
            else:
                before = x_row(c0, c - 1, f, 31)
            after = jnp.where(at_end, high, edge[3, f])
            if c < CAP - 1:
                after = jnp.where(last, after, x_row(c0, c + 1, f, 0))
            set_x_ghost(c0, c, f, before, after)

    def coarse_step(s, _):
        def emit(r, j, f, v):
            c1[s, f, pl.ds(32 * j + 8 * r, 8), :] = v

        step(c0, s, cl, s, s, mat, emit)
        return 0

    lax.fori_loop(0, CAP, coarse_step, 0)
    for copy in regs:
        copy.wait()

    def take(i, _):
        reg[OLD + i] = rinbox[i]
        return 0

    lax.fori_loop(0, plan.reg_pool - OLD, take, 0)
    right_half = (wide % 32) >= 16
    for c in range(CAP):
        for face in range(2):
            mine = [x_row(c0, c, f, 31 * face) for f in range(5)]
            ghost = [x_row(c0, c, f, 32 if face else -1) for f in range(5)]
            flux = face_flux(mine, ghost, 0) if face else face_flux(ghost, mine, 0)
            for half in range(2):
                k = 44 + c * 8 + face * 4 + half * 2
                has = jnp.where(right_half, tab[k + 1], tab[k]) >= 0
                i0, i1 = jnp.maximum(tab[k], 0), jnp.maximum(tab[k + 1], 0)
                sums = []
                for f in range(5):
                    rows = pl.ds(4 * f, 4)
                    sums.append(0.125 * jnp.where(right_half, reg[i1, rows, :], reg[i0, rows, :]))
                speed = background[0]
                value = [
                    speed * sums[0] + sums[1],
                    speed * sums[1] + sums[4],
                    speed * sums[2],
                    speed * sums[3],
                    speed * sums[4] + sound_sq * sums[1],
                ]
                for f in range(5):
                    tmp[f] = flux[f]
                    part = tmp[f, pl.ds(4 * half, 4), :]
                    rows = pl.ds(128 * half + 31 * face, 4, stride=32)
                    fix = courant * (value[f] - part)
                    fix = -fix if face else fix
                    c1[c, f, rows, :] = c1[c, f, rows, :] + jnp.where(has, fix, 0.0)
    for j in range(8):
        copy = pltpu.make_async_copy(
            c1.at[:, :, pl.ds(32 * j, 32), :], cnew.at[:, :, :, pl.ds(128 * j, 128)], dsem.at[j]
        )
        copy.start()
        stores.append(copy)
    for copy in stores:
        copy.wait()
    for copy in moves:
        copy.wait()


def body_two(tab, mig, cnew, coarse_out, fine_new, held, zeros, in_sem, out_sem):
    jobs = [(c, tab[NEW] > c, c, cnew, coarse_out) for c in range(CAP)]
    jobs += [(CAP + n, tab[n] >= 0, tab[n], mig, fine_new) for n in range(NEW)]
    for k, live, idx, src, _ in jobs:

        @pl.when(live)
        def _():
            pltpu.make_async_copy(src.at[idx], held.at[k], in_sem.at[k]).start()

    def clear(f, _):
        for r in range(4):
            zeros[f, pl.ds(8 * r, 8), :] = jnp.zeros((8, 1024), jnp.float32)
        return 0

    lax.fori_loop(0, 5, clear, 0)

    def target(k, dst):
        return dst.at[k if k < CAP else k - CAP]

    for k, live, idx, src, dst in jobs:

        @pl.when(jnp.logical_not(live))
        def _():
            pltpu.make_async_copy(zeros, target(k, dst), out_sem.at[k]).start()

    for k, live, idx, src, dst in jobs:

        @pl.when(live)
        def _():
            pltpu.make_async_copy(src.at[idx], held.at[k], in_sem.at[k]).wait()
            pltpu.make_async_copy(held.at[k], target(k, dst), out_sem.at[k]).start()

    for k, live, idx, src, dst in jobs:
        pltpu.make_async_copy(zeros, target(k, dst), out_sem.at[k]).wait()


TO_PEER = 72


def fill_tables(plan, me, own_old, own_new, own_crs, nbr, flux_map, tab, tab2):
    def start(owners, mark):
        return jnp.sum((owners[...] < mark).astype(jnp.int32))

    old = [start(own_old, me + k) for k in range(-3, 5)]
    new = [start(own_new, me + k) for k in range(2)]
    crs = [start(own_crs, me + k) for k in range(2)]
    total = own_old.shape[0] * own_old.shape[1]
    base, end = old[3], old[4]
    cut, cut_end = base % 8, end % 8
    prev1, next1 = OLD, OLD + plan.one
    prev2, next2 = OLD + 2 * plan.one, OLD + 2 * plan.one + plan.two

    def patch(p):
        p = jnp.clip(p, 0, total - 1)
        return jnp.maximum(nbr[0, p], nbr[1, p]), nbr[2, p], nbr[4, p]

    def spot(p, u):
        where = u - base
        before = prev1 + jnp.where(cut <= 4, u - (base - cut), p - base)
        after = next1 + jnp.where(cut_end <= 4, p - (end - cut_end), u - end)
        where = jnp.where(u < base, before, where)
        where = jnp.where(u < old[2], prev2, where)
        where = jnp.where(u >= end, after, where)
        where = jnp.where(u >= old[5], next2, where)
        return jnp.clip(where, 0, plan.pool - 1)

    def one_patch(s, _):
        p = base + s
        nx, ny, nz = patch(p)
        tab[s] = spot(p, nx)
        tab[10 + s] = spot(p, ny)
        tab[20 + s] = spot(p, nz)
        return 0

    def one_side(s, _):
        p = base + s
        tab[30 + s] = (nbr[0, jnp.clip(p, 0, total - 1)] >= 0).astype(jnp.int32)
        return 0

    lax.fori_loop(0, OLD, one_side, 0)
    tab[40] = end - base
    tab[41] = crs[1] - crs[0]
    tab[42] = (crs[0] == 0).astype(jnp.int32)
    tab[43] = (crs[1] == 2 * own_crs.shape[1]).astype(jnp.int32)

    def local(u):
        return jnp.clip(u - base, 0, OLD - 1)

    def to_peers(i, _):
        own = local(end - cut_end + i)
        parts = patch(end + i)
        for k in range(3):
            tab[TO_PEER + 3 * i + k] = jnp.where(cut_end <= 4, own, local(parts[k]))
        parts = patch(base - cut + i)
        for k in range(3):
            at = TO_PEER + 3 * (plan.one + i) + k
            tab[at] = jnp.where(cut <= 4, local(parts[k]), local(base + i))
        return 0

    lax.fori_loop(0, plan.one, to_peers, 0)
    for i in range(plan.two):
        for k in range(3):
            at = TO_PEER + 3 * (2 * plan.one + i) + k
            tab[at] = local(end - plan.two + i)
            tab[at + 3 * plan.two] = local(base + i)

    def reg_spot(p):
        where = p - base
        at = OLD
        for k, w in plan.reg_windows:
            where = jnp.where(p < old[4 - k], at + w - (old[4 - k] - p), where)
            where = jnp.where(p >= old[3 + k], at + w + (p - old[3 + k]), where)
            at += 2 * w
        return jnp.clip(where, 0, at - 1)

    def one_face(e, _):
        c, face = e // 2, e % 2
        g = crs[0] + c
        block = (g + 1) // 2 - 1 + face
        live = g < crs[1]
        found = [jnp.int32(-1)] * 4
        for i in range(8):
            p = jnp.clip(8 * block + i, 0, total - 1)
            hit = live & (flux_map[0, p] == g) & (flux_map[1, p] == face)
            place = reg_spot(p)
            quarter = flux_map[2, p]
            for q in range(4):
                found[q] = jnp.where(hit & (quarter == q), place, found[q])
        for q in range(4):
            tab[44 + 4 * e + q] = found[q]
        return 0

    def one_row(n, _):
        p = new[0] + n
        src = p - base
        src = jnp.where(p < base, OLD + 2 - (base - p), src)
        src = jnp.where(p >= end, OLD + 2 + (p - end), src)
        tab2[n] = jnp.where(p < new[1], jnp.clip(src, 0, OLD + 3), -1)
        return 0

    def place():
        lax.fori_loop(0, OLD, one_patch, 0)

    def late():
        lax.fori_loop(0, 2 * CAP, one_face, 0)
        lax.fori_loop(0, NEW, one_row, 0)
        tab2[NEW] = crs[1] - crs[0]

    return place, late


def cuts_body(own_old, own_crs, flux_map, wide_out, target_rows):
    owner = own_old[...]
    lane = lane_ids()
    for j in range(8):
        target_rows[pl.ds(j, 1), :] = flux_map[pl.ds(0, 1), pl.ds(128 * j, 128)]
    target = target_rows[...]

    def moved(lane_shift, row_shift, edge):
        turned = pltpu.roll(owner, lane_shift, 1)
        return jnp.where(lane == edge, pltpu.roll(turned, row_shift, 0), turned)

    first, last = moved(1, 1, 0) != owner, moved(127, 7, 127) != owner
    cut = lane % 8
    wide = first & (cut >= 2) & (cut <= 6)
    spot = jnp.maximum(target, 0) % 128
    onto = [pick(jnp.broadcast_to(own_crs[pl.ds(k, 1), :], (8, 128)), spot) for k in range(2)]
    away = jnp.where(target >= 0, jnp.where(target < 128, onto[0], onto[1]) - owner, 0)
    far = (jnp.abs(away) > 2) | ((away == 2) & ~last) | ((away == -2) & ~first)
    wide_out[0] = jnp.max(jnp.where(wide | far, 1, 0))


def cuts(owners, flux_map):
    vmem = pl.BlockSpec(memory_space=pltpu.VMEM)
    return pl.pallas_call(
        cuts_body,
        name="cuts",
        out_shape=jax.ShapeDtypeStruct((1,), jnp.int32),
        in_specs=[vmem] * 3,
        out_specs=pl.BlockSpec(memory_space=pltpu.SMEM),
        scratch_shapes=[pltpu.VMEM((8, 128), jnp.int32)],
    )(owners[0], owners[2], flux_map)


def stage_one(plan, number, n_grp, n_sfc, owners, nbr, flux_map, fine, coarse):
    f32 = jnp.float32
    big = pl.BlockSpec(memory_space=pl.ANY)
    smem = pl.BlockSpec(memory_space=pltpu.SMEM)
    vmem = pl.BlockSpec(memory_space=pltpu.VMEM)
    tall = 8 * PITCH
    wide_stage = plan.pool - OLD
    return pl.pallas_call(
        functools.partial(body_one, plan, n_grp, n_sfc),
        name="advance_level",
        out_shape=(
            jax.ShapeDtypeStruct((OLD + 4, 5, 32, 1024), f32),
            jax.ShapeDtypeStruct((CAP, 5, 32, 1024), f32),
            jax.ShapeDtypeStruct((16,), jnp.int32),
        ),
        in_specs=[vmem] * 3 + [smem] * 2 + [big, big],
        out_specs=(big, big, smem),
        scratch_shapes=[
            pltpu.VMEM((OLD, 5, tall, 128), f32),
            pltpu.VMEM((OLD, 5, tall, 128), f32),
            pltpu.VMEM((OLD, 5, 32, 1024), f32),
            pltpu.VMEM((CAP, 5, tall, 128), f32),
            pltpu.VMEM((CAP, 5, 256, 128), f32),
            pltpu.VMEM((CAP, 5, 32, 128), f32),
            pltpu.VMEM((plan.pool, 5, 40, 128), f32),
            pltpu.VMEM((plan.pool, 5, 40, 128), f32),
            pltpu.VMEM((2, wide_stage, 5, 40, 128), f32),
            pltpu.VMEM((2, wide_stage, 5, 40, 128), f32),
            pltpu.VMEM((plan.reg_pool, 24, 128), f32),
            pltpu.VMEM((plan.reg_pool - OLD, 24, 128), f32),
            pltpu.VMEM(((plan.reg_pool - OLD) // 2, 24, 128), f32),
            pltpu.VMEM((4, 5, 8, 128), f32),
            pltpu.VMEM((2, 5, 32, 1024), f32),
            pltpu.VMEM((5, 8, 128), f32),
            pltpu.SMEM((128,), jnp.int32),
            pltpu.VMEM((256, 256), jnp.bfloat16),
            pltpu.SemaphoreType.DMA((24,)),
            pltpu.SemaphoreType.DMA((24,)),
            pltpu.SemaphoreType.DMA((24,)),
        ],
        compiler_params=pltpu.CompilerParams(
            collective_id=number, has_side_effects=True, vmem_limit_bytes=58 * 2**20
        ),
    )(*owners, nbr, flux_map, fine, coarse)


def stage_two(tab, mig, cnew):
    f32 = jnp.float32
    big = pl.BlockSpec(memory_space=pl.ANY)
    return pl.pallas_call(
        body_two,
        name="place_patches",
        out_shape=(
            jax.ShapeDtypeStruct((CAP, 5, 32, 1024), f32),
            jax.ShapeDtypeStruct((NEW, 5, 32, 1024), f32),
        ),
        in_specs=[pl.BlockSpec(memory_space=pltpu.SMEM), big, big],
        out_specs=(big, big),
        scratch_shapes=[
            pltpu.VMEM((CAP + NEW, 5, 32, 1024), f32),
            pltpu.VMEM((5, 32, 1024), f32),
            pltpu.SemaphoreType.DMA((CAP + NEW,)),
            pltpu.SemaphoreType.DMA((CAP + NEW,)),
        ],
        compiler_params=pltpu.CompilerParams(vmem_limit_bytes=58 * 2**20),
    )(tab, mig, cnew)


def solution(mesh):
    n_grp, n_sfc = mesh.shape["grp"], mesh.shape["sfc"]
    common, general = Plan(1, 1, (10, 1)), Plan(4, 1, (10, 10, 10))

    def body(coarse_state, fine_old, coarse_owner, owner_old, owner_new, nbr, reflux):
        owners = (owner_old.reshape(8, -1), owner_new.reshape(8, -1), coarse_owner.reshape(2, -1))
        args = (owners, nbr.T, reflux.T, fine_old, coarse_state)
        mig, cnew, tab = lax.cond(
            cuts(owners, reflux.T)[0] == 0,
            functools.partial(stage_one, common, 0, n_grp, n_sfc),
            functools.partial(stage_one, general, 1, n_grp, n_sfc),
            *args,
        )
        return stage_two(tab, mig, cnew)

    split = P(("grp", "sfc"), None, None, None)
    return jax.shard_map(
        body,
        mesh=mesh,
        in_specs=(split, split, P(), P(), P(), P(), P()),
        out_specs=(split, split),
        check_vma=False,
    )
```
